128 devices in a mesh: view: 2 (over z_lo), fx: 4 (over y), fy: 16 (over x, z_hi, core).
Axes of the slice: x: 4, y: 4, z: 4 (z_hi: 2, z_lo: 2; z = z_hi * 2 + z_lo), core: 2. Of those that a mesh axis runs over, the one named last changes fastest.
Arguments:
- estimate: float32 [128, 512, 128], P('fx', 'fy'), may hold values from 0.25 to 30
- images: bfloat16 [6, 128, 512, 128], P('view', 'fx', 'fy'), may hold values from 0.1 to 30
- psf: float32 [6, 3, 31], P('view'), may hold values from 0.05 to 1
- cover_lo: int32 [6, 4, 16], P('view'), may hold values from 0 to 63
- cover_len: int32 [6, 4, 16], P('view'), may hold values from 32 to 64
Outputs:
- joined: float32 [128, 512, 128], P('fx', 'fy')
The draws below stay inside these ranges and needn't reach their ends.
All inputs are finite; a program needn't handle non-finite values.
Results may differ from the reference program's by a relative error of at most 0.0003.
Values may be sent and summed in bfloat16 or wider, within the bound.
A program may use at most 64 MiB of HBM per device.

```python
import math
import jax
import jax.numpy as jnp
from jax import lax

CX = 32
CY = 32
NZ = 128
VIEWS = 6
TAPS = 31
ITERS = 2
GX = 4
GY = 16
NX = 128
NY = 512


def smooth_part(subkey, strength):
    phases = jax.random.uniform(subkey, (2, 3), jnp.float32)
    cycles = 1.0 + phases[0]
    pos_x = jnp.arange(NX, dtype=jnp.float32) / NX
    pos_y = jnp.arange(NY, dtype=jnp.float32) / NY
    pos_z = jnp.arange(NZ, dtype=jnp.float32) / NZ
    wave_x = jnp.cos(2.0 * math.pi * (cycles[0] * pos_x + phases[1, 0]))
    wave_y = jnp.cos(2.0 * math.pi * (cycles[1] * pos_y + phases[1, 1]))
    wave_z = jnp.cos(2.0 * math.pi * (cycles[2] * pos_z + phases[1, 2]))
    summed = wave_x[:, None, None] + wave_y[None, :, None] + wave_z[None, None, :]
    return jnp.exp(strength * summed)


def expand_cells(table, cell_side):
    grown = jnp.repeat(jnp.repeat(jnp.repeat(table, cell_side, axis=0), cell_side, axis=1), cell_side, axis=2)
    return grown[:NX, :NY, :NZ]


def blob_part(subkey, bright_lo, bright_hi):
    cell_side = 16
    cell_counts = ((NX + cell_side - 1) // cell_side, (NY + cell_side - 1) // cell_side, (NZ + cell_side - 1) // cell_side)
    subkeys = jax.random.split(subkey, 4)
    centres = jax.random.uniform(subkeys[0], cell_counts + (3,), jnp.float32, 5.0, 11.0)
    radius = jnp.exp(jax.random.uniform(subkeys[1], cell_counts, jnp.float32, 0.0, math.log(3.0)))
    bright = jnp.exp(jax.random.uniform(subkeys[2], cell_counts, jnp.float32, math.log(bright_lo), math.log(bright_hi)))
    lit_cells = jax.random.bernoulli(subkeys[3], 0.5, cell_counts)
    levels = jnp.where(lit_cells, bright, jnp.zeros_like(bright))
    offset_x = (jnp.arange(NX, dtype=jnp.int32) % cell_side).astype(jnp.float32)
    offset_y = (jnp.arange(NY, dtype=jnp.int32) % cell_side).astype(jnp.float32)
    offset_z = (jnp.arange(NZ, dtype=jnp.int32) % cell_side).astype(jnp.float32)
    dist_sq = (offset_x[:, None, None] - expand_cells(centres[..., 0], cell_side)) ** 2
    dist_sq = dist_sq + (offset_y[None, :, None] - expand_cells(centres[..., 1], cell_side)) ** 2
    dist_sq = dist_sq + (offset_z[None, None, :] - expand_cells(centres[..., 2], cell_side)) ** 2
    spread = expand_cells(radius, cell_side)
    return expand_cells(levels, cell_side) * jnp.exp(-dist_sq / (2.0 * spread * spread))


def structured_volume(subkey, noise_lo, noise_hi):
    subkeys = jax.random.split(subkey, 3)
    smooth = smooth_part(subkeys[0], 0.12)
    noise = jnp.exp(jax.random.uniform(subkeys[1], (NX, NY, NZ), jnp.float32, math.log(noise_lo), math.log(noise_hi)))
    blobs = blob_part(subkeys[2], 3.0, 10.0)
    return smooth * (noise + blobs)


def draw_estimate(key, part):
    return structured_volume(jax.random.fold_in(key, 11), 0.5, 2.0)


def draw_images(key, part):
    view_keys = jax.random.split(jax.random.fold_in(key, 23), VIEWS)

    def one_view(view_key):
        return structured_volume(view_key, 0.25, 4.0).astype(jnp.bfloat16)
    return jax.lax.map(one_view, view_keys)


def place_ends(result, rng, least, top_value):
    index_at = [jax.random.randint(jax.random.fold_in(rng, axis), (), 0, length) for axis, length in enumerate(result.shape)]
    longest = result.shape.index(max(result.shape))
    next_to = index_at[:longest] + [(index_at[longest] + 1) % result.shape[longest]] + index_at[longest + 1:]
    return result.at[tuple(index_at)].set(least).at[tuple(next_to)].set(top_value)


def level_of(rng, shape, pieces, least, largest):
    loudness = 1.0
    for position, blocks in pieces:
        draws = jax.random.uniform(jax.random.fold_in(jax.random.fold_in(rng, 6), position), (blocks,), jnp.float32, least / len(pieces), largest / len(pieces))
        loudness = loudness * jnp.repeat(jnp.exp(draws), shape[position] // blocks).reshape((-1,) + (1,) * (len(shape) - 1 - position))
    return loudness


def setup_inputs(seed: int = 0) -> dict:
    streams_of = jax.random.split(jax.random.key(seed), 6)
    return {
        "estimate": draw_estimate(jax.random.fold_in(streams_of[5], 71), 0),
        "images": draw_images(jax.random.fold_in(streams_of[5], 71), 0),
        "psf": jnp.clip(jnp.exp(math.log(1.0) - 2.9957323 * jax.random.uniform(streams_of[2], (VIEWS, 3, TAPS), jnp.float32) ** level_of(streams_of[2], (VIEWS, 3, TAPS), ((0, 2),), -0.2, 0.2)), 0.05, 1.0),
        "cover_lo": place_ends(jax.random.randint(streams_of[3], (VIEWS, GX, GY), 0, NZ // 2), jax.random.fold_in(streams_of[3], 1), 0, (NZ // 2) - 1).astype(jnp.int32),
        "cover_len": place_ends(jax.random.randint(streams_of[4], (VIEWS, GX, GY), NZ // 4, NZ // 2 + 1), jax.random.fold_in(streams_of[4], 1), NZ // 4, (NZ // 2 + 1) - 1).astype(jnp.int32),
    }


def blur_axis(field, weights, axis, backward):
    taps = weights.shape[0]
    radius = (taps - 1) // 2
    widths = [(0, 0), (0, 0), (0, 0)]
    widths[axis] = (radius, radius)
    padded = jnp.pad(field, widths)
    length = field.shape[axis]
    total = jnp.zeros(field.shape, jnp.float32)
    for tap in range(taps):
        start = taps - 1 - tap if backward else tap
        total = total + weights[tap] * lax.slice_in_dim(padded, start, start + length, axis=axis)
    return total


def blur_all(field, weights, backward):
    for axis in range(3):
        field = blur_axis(field, weights[axis], axis, backward)
    return field


def reference(estimate, images, psf, cover_lo, cover_len):
    kern = psf / jnp.sum(psf, axis=-1, keepdims=True)
    depth = jnp.arange(NZ, dtype=jnp.int32)
    masked = []
    weight = jnp.zeros(estimate.shape, jnp.float32)
    for view in range(VIEWS):
        low = jnp.repeat(jnp.repeat(cover_lo[view], CX, axis=0), CY, axis=1)
        span = jnp.repeat(jnp.repeat(cover_len[view], CX, axis=0), CY, axis=1)
        inside = (depth >= low[:, :, None]) & (depth < (low + span)[:, :, None])
        weight = weight + blur_all(inside.astype(jnp.float32), kern[view], True)
        masked.append(jnp.where(inside, images[view], jnp.zeros_like(images[view])))
    joined = estimate
    for step in range(ITERS):
        correction = jnp.zeros(estimate.shape, jnp.float32)
        for view in range(VIEWS):
            blurred = blur_all(joined, kern[view], False)
            ratio = masked[view].astype(jnp.float32) / blurred
            correction = correction + blur_all(ratio, kern[view], True)
        joined = joined * (correction + 0.5) / (weight + 0.5)
    return joined
```

```python
import functools

import jax
import jax.numpy as jnp
from jax import lax
from jax.experimental import pallas as pl
from jax.experimental.pallas import tpu as pltpu
from jax.sharding import PartitionSpec as P

ITERS = 2
MESH = pl.DeviceIdType.MESH
BF16 = jnp.bfloat16
F32 = jnp.float32
I16 = jnp.int16
QMAX = 32000.0

DIRS = tuple((dy, dx) for dy in (-1, 0, 1) for dx in (-1, 0, 1) if dy or dx)
INDEX = {d: i for i, d in enumerate(DIRS)}
SEND_ORDER = ((1, 0), (-1, 0), (1, 1), (1, -1), (-1, 1), (-1, -1), (0, 1), (0, -1))

E_SRC_Y = {1: (33, 15), -1: (16, 15), 0: (16, 32)}
E_DST_Y = {-1: (1, 15), 1: (48, 15), 0: (16, 32)}
E_SRC_X = {1: (32, 16), -1: (16, 16), 0: (16, 32)}
E_DST_X = {-1: (0, 16), 1: (48, 16), 0: (16, 32)}
C_SRC_Y = {1: (48, 15), -1: (1, 15), 0: (16, 32)}
C_SRC_X = {1: (48, 16), -1: (0, 16), 0: (16, 32)}


def dot(a, b):
    return jnp.dot(a, b, preferred_element_type=F32)


def split(v):
    hi = v.astype(BF16)
    return hi, (v - hi.astype(F32)).astype(BF16)


def kernel(
    fx_size, fy_size,
    est_ref, img_ref, psf_ref, lo_ref, len_ref, out_ref,
    ext, joined, img2, kern, masks, wide_a, wide_b, corr, quant,
    got_x, got_y, got_c, scale, got_scale,
    fxt, fyt, fzt, bzt, byt, bxh, bxl, low_inv, mz, txs, tys, tpose,
    e_send, e_recv, c_send, c_recv, s_send, s_recv, v_send, v_recv,
):
    g = lax.axis_index("view")
    bx = lax.axis_index("fx")
    by = lax.axis_index("fy")
    core = lax.rem(by, 2)
    own = g * 3
    oth = 3 - own

    def exists(d):
        dy, dx = d
        ok = jnp.bool_(True)
        if dy:
            ok = ok & (by + dy >= 0) & (by + dy < fy_size)
        if dx:
            ok = ok & (bx + dx >= 0) & (bx + dx < fx_size)
        return ok

    def peer(d):
        dy, dx = d
        cross = core if dy == 1 else (1 - core if dy == -1 else 0)
        return (g + cross - 2 * g * cross, bx + dx, by + dy)

    partner = (1 - g, bx, by)

    def ext_copy(d):
        s = (-d[0], -d[1])
        ys, ny = E_SRC_Y[d[0]]
        xs, nx = E_SRC_X[d[1]]
        yd, _ = E_DST_Y[s[0]]
        xd, _ = E_DST_X[s[1]]
        return pltpu.make_async_remote_copy(
            ext.at[pl.ds(ys, ny), pl.ds(xs, nx), :],
            ext.at[pl.ds(yd, ny), pl.ds(xd, nx), :],
            e_send.at[INDEX[d]], e_recv.at[INDEX[s]],
            device_id=peer(d), device_id_type=MESH)

    def landing(s):
        if s[0] == 0:
            return got_x.at[(s[1] + 1) // 2]
        if s[1] == 0:
            return got_y.at[(s[0] + 1) // 2]
        return got_c.at[(s[0] + 1) // 2, (s[1] + 1) // 2]

    def corr_copies(d):
        s = (-d[0], -d[1])
        ys, ny = C_SRC_Y[d[0]]
        xs, nx = C_SRC_X[d[1]]
        return (
            pltpu.make_async_remote_copy(
                scale, got_scale.at[INDEX[s]],
                s_send.at[INDEX[d]], s_recv.at[INDEX[s]],
                device_id=peer(d), device_id_type=MESH),
            pltpu.make_async_remote_copy(
                quant.at[pl.ds(ys, ny), pl.ds(xs, nx), :], landing(s),
                c_send.at[INDEX[d]], c_recv.at[INDEX[s]],
                device_id=peer(d), device_id_type=MESH),
        )

    def each(order, action):
        for d in order:
            @pl.when(exists(d))
            def _(d=d):
                action(d)

    def send_ext():
        each(SEND_ORDER, lambda d: ext_copy(d).start())

    ext[...] = jnp.zeros_like(ext)

    def load_est(y, _):
        row = est_ref[pl.ds(y, 32, stride=32), :]
        joined[pl.ds(pl.multiple_of(y * 32, 32), 32), :] = row
        ext[pl.ds(y + 16, 1), 16:48, :] = row.astype(BF16)[None]
        return 0

    lax.fori_loop(0, 32, load_est, 0)

    kern[...] = jnp.zeros_like(kern)
    lane = lax.broadcasted_iota(jnp.int32, (16, 128), 1)
    row16 = lax.broadcasted_iota(jnp.int32, (16, 128), 0)
    for k in range(3):
        taps = psf_ref[k]
        kern[pl.ds(own + k, 1), 0:3, 0:31] = (taps / jnp.sum(taps, axis=-1, keepdims=True))[None]
        low = jnp.zeros((16, 128), jnp.int32)
        top = jnp.zeros((16, 128), jnp.int32)
        for jy in range(3):
            for jx in range(3):
                px = bx + (jx - 1)
                py = by + (jy - 1)
                inside = (px >= 0) & (px < fx_size) & (py >= 0) & (py < fy_size)
                cx = jnp.clip(px, 0, fx_size - 1)
                cy = jnp.clip(py, 0, fy_size - 1)
                here = row16 == jy * 3 + jx
                start = lo_ref[k, cx, cy]
                span = len_ref[k, cx, cy] * inside.astype(jnp.int32)
                low = jnp.where(here, start, low)
                top = jnp.where(here, start + span, top)
        masks[pl.ds(own + k, 1)] = jnp.where(
            (lane >= low) & (lane < top), 1.0, 0.0).astype(BF16)[None]

    barrier = pltpu.get_barrier_semaphore()
    count = jnp.int32(1)
    for d in DIRS:
        count = count + exists(d).astype(jnp.int32)
    pl.semaphore_signal(barrier, inc=1, device_id=partner, device_id_type=MESH)
    each(DIRS, lambda d: pl.semaphore_signal(
        barrier, inc=1, device_id=peer(d), device_id_type=MESH))
    pl.semaphore_wait(barrier, count)

    send_ext()
    kern_copy = pltpu.make_async_remote_copy(
        kern.at[pl.ds(own, 3)], kern.at[pl.ds(own, 3)],
        v_send.at[3], v_recv.at[3], device_id=partner, device_id_type=MESH)
    mask_copy = pltpu.make_async_remote_copy(
        masks.at[pl.ds(own, 3)], masks.at[pl.ds(own, 3)],
        v_send.at[4], v_recv.at[4], device_id=partner, device_id_type=MESH)

    def img_copy(i):
        return pltpu.make_async_remote_copy(
            img_ref.at[i], img2.at[i], v_send.at[i], v_recv.at[i],
            device_id=partner, device_id_type=MESH)

    kern_copy.start()
    mask_copy.start()
    for i in range(3):
        img_copy(i).start()

    for d in DIRS:
        @pl.when(jnp.logical_not(exists(d)))
        def _(d=d):
            ref = landing(d)
            ref[...] = jnp.zeros(ref.shape, I16)
            got_scale[INDEX[d]] = jnp.zeros((8, 128), F32)

    kern_copy.wait()
    mask_copy.wait()

    zr = lax.broadcasted_iota(jnp.int32, (128, 128), 0)
    zc = lax.broadcasted_iota(jnp.int32, (128, 128), 1)
    near = (zc - zr <= 15) & (zr - zc <= 15)
    mz[...] = jnp.zeros_like(mz)

    def banded(row):
        return pltpu.roll(jnp.broadcast_to(row, (32, 128)), 1, 1, stride=1, stride_axis=0)

    lane32 = lax.broadcasted_iota(jnp.int32, (32, 128), 1)
    pos32 = lax.broadcasted_iota(jnp.int32, (32, 128), 0)

    def side_sums(row):
        taps = jnp.broadcast_to(row, (32, 128))
        before = jnp.sum(jnp.where(lane32 >= pos32 + 16, taps, 0.0), axis=1, keepdims=True)
        after = jnp.sum(jnp.where(lane32 <= pos32 - 17, taps, 0.0), axis=1, keepdims=True)
        middle = jnp.sum(
            jnp.where((lane32 < pos32 + 16) & (lane32 > pos32 - 17), taps, 0.0),
            axis=1, keepdims=True)
        return before, middle, after

    def tables(k, carry):
        sums_x, sums_y = carry
        rows = kern[k]
        tx = banded(rows[0:1])
        ty = banded(rows[1:2])
        xh, xl = split(tx)
        yh, yl = split(ty)
        r = pl.multiple_of(k * 32, 32)
        fxt[pl.ds(r, 32), :] = (
            xh.astype(F32) + pltpu.roll(xl.astype(F32), 64, 1)).astype(BF16)
        fyt[k] = (yh.astype(F32) + pltpu.roll(yl.astype(F32), 64, 1)).astype(BF16)
        tpose[pl.ds(r, 32), :] = xh.astype(F32)
        tpose[pl.ds(r + 256, 32), :] = xl.astype(F32)
        both = jnp.concatenate(
            [yh.astype(F32), yl.astype(F32), jnp.zeros((64, 128), F32)], axis=0)
        byt[k] = both.T[0:64, :].astype(BF16)
        tz = pltpu.roll(
            jnp.broadcast_to(rows[2:3], (128, 128)), 113, 1, stride=1, stride_axis=0)
        tz = jnp.where(near, tz, 0.0)
        bh, bl = split(tz)
        bzt[k, 0:128] = bh
        bzt[k, 128:256] = bl
        fh, fl = split(tz.T)
        fzt[k, 0:128] = fh
        fzt[k, 128:256] = fl
        m = masks[k]
        mz[pl.ds(pl.multiple_of(k * 16, 16), 16), :] = dot(
            jnp.concatenate([m, m], axis=1), bzt[k])
        part = lane32 - k * 16
        mine = (part >= 0) & (part < 9)
        px = lax.rem(part + 96, 3)
        py = (part + 96) // 3 - 32
        for j, col in enumerate(side_sums(rows[0:1])):
            sums_x = jnp.where(mine & (px == j), col, sums_x)
        for j, col in enumerate(side_sums(rows[1:2])):
            sums_y = jnp.where(mine & (py == j), col, sums_y)
        return sums_x, sums_y

    zero = jnp.zeros((32, 128), F32)
    sums_x, sums_y = lax.fori_loop(0, 6, tables, (zero, zero))
    txs[...] = sums_x
    tys[...] = sums_y
    for half in range(2):
        a = tpose[0:128, :].T if half == 0 else tpose[256:384, :].T
        b = (tpose[128:192, :] if half == 0 else tpose[384:448, :])
        b = jnp.concatenate([b, jnp.zeros((64, 128), F32)], axis=0).T
        ref = bxh if half == 0 else bxl
        ref[:, 0:128] = a[0:64].astype(BF16)
        ref[:, 128:256] = b[0:64].astype(BF16)

    def weigh(q, _):
        parts = []
        for j in range(8):
            parts.append(txs[...] * tys[pl.ds(q * 8 + j, 1), :])
        w = jnp.dot(jnp.concatenate(parts, axis=0), mz[...],
                    preferred_element_type=F32, precision=lax.Precision.HIGHEST)
        low_inv[pl.ds(pl.multiple_of(q * 256, 256), 256), :] = 1.0 / (w + 0.5)
        return 0

    lax.fori_loop(0, 4, weigh, 0)

    def view_step(k, images, q):
        covered = masks[k, 4:5, :].astype(F32) > 0.5
        ty = fyt[k]
        blurred = []
        for p in range(4):
            pair = []
            for j in range(2):
                r = k * 32 + q * 8 + (p * 2 + j)
                pair.append(wide_a[pl.ds(r, 64, stride=192), :].astype(BF16))
            cols = jnp.concatenate(pair, axis=1)
            out = dot(ty, jnp.concatenate([cols, cols], axis=0))
            blurred += [out[:, 0:128], out[:, 128:256]]
        u = jnp.concatenate(blurred, axis=0).astype(BF16)
        f = dot(jnp.concatenate([u, u], axis=1), fzt[k])
        pic = images[pl.ds(pl.multiple_of(q * 256, 256), 256), :].astype(F32)
        ratio = (jnp.where(covered, pic, 0.0) / f).astype(BF16)
        v = dot(jnp.concatenate([ratio, ratio], axis=1), bzt[k]).astype(BF16)
        back = byt[k][:, 0:64]
        for p in range(4):
            a = v[p * 64:p * 64 + 32]
            b = v[p * 64 + 32:p * 64 + 64]
            cols = jnp.concatenate([a, b], axis=1)
            out = dot(back, jnp.concatenate([cols, cols], axis=0))
            for j in range(2):
                r = (k * 32 + q * 8 + (p * 2 + j)) * 64
                wide_b[pl.ds(pl.multiple_of(r, 64), 64), :] = out[:, j * 128:j * 128 + 128]

    for step in range(ITERS):
        each(DIRS, lambda d: recv_ext(ext_copy, d))

        def pass_x(p, _):
            cols = jnp.concatenate([ext[p * 2], ext[p * 2 + 1]], axis=1)
            out = dot(fxt[...], jnp.concatenate([cols, cols], axis=0))
            for j in range(2):
                r = pl.multiple_of((p * 2 + j) * 192, 192)
                wide_a[pl.ds(r, 192), :] = out[:, j * 128:j * 128 + 128]
            return 0

        lax.fori_loop(0, 32, pass_x, 0)

        def own_views(n, _):
            view_step(own + n // 4, img_ref.at[n // 4], lax.rem(n, 4))
            return 0

        lax.fori_loop(0, 12, own_views, 0)

        if step == 0:
            for i in range(3):
                img_copy(i).wait()

        def other_views(n, _):
            view_step(oth + n // 4, img2.at[n // 4], lax.rem(n, 4))
            return 0

        lax.fori_loop(0, 12, other_views, 0)

        def back_x(p, peak):
            pair = [wide_b[pl.ds(p * 2 + j, 192, stride=64), :] for j in range(2)]
            hi, lo = split(jnp.concatenate(pair, axis=1))
            th = bxh[:, 0:192]
            out = dot(th, hi) + (dot(th, lo) + dot(bxl[:, 0:192], hi))
            for j in range(2):
                part = out[:, j * 128:j * 128 + 128]
                corr[p * 2 + j] = part
                peak = jnp.maximum(peak, part)
            return peak

        peak = lax.fori_loop(0, 32, back_x, jnp.zeros((64, 128), F32))
        peak = jnp.max(jnp.max(peak, axis=0, keepdims=True), axis=1, keepdims=True)
        peak = jnp.maximum(peak, 1e-30)

        if step > 0:
            each(DIRS, lambda d: [c.wait_send() for c in corr_copies(d)])
        scale[...] = jnp.broadcast_to(peak * (1.0 / QMAX), (8, 128))
        gain = jnp.broadcast_to(QMAX / peak, (64, 128))

        def code(y, _):
            quant[y] = jnp.round(corr[y] * gain).astype(jnp.int32).astype(I16)
            return 0

        lax.fori_loop(1, 63, code, 0)
        each(SEND_ORDER, lambda d: [c.start() for c in corr_copies(d)])
        each(DIRS, lambda d: ext_copy(d).wait_send())
        each(DIRS, lambda d: recv_corr(corr_copies, d))

        factors = {d: jnp.broadcast_to(got_scale[INDEX[d], 0:1, :], (16, 128)) for d in DIRS}

        def wide(ref):
            return ref.astype(jnp.int32).astype(F32)

        def finish(y, i, sy):
            left = corr[y + 16, 16:32, :] + wide(got_x[0, y]) * factors[(0, -1)]
            right = corr[y + 16, 32:48, :] + wide(got_x[1, y]) * factors[(0, 1)]
            if sy:
                s = (sy + 1) // 2
                left = left + wide(got_y[s, i, 0:16]) * factors[(sy, 0)]
                left = left + wide(got_c[s, 0, i]) * factors[(sy, -1)]
                right = right + wide(got_y[s, i, 16:32]) * factors[(sy, 0)]
                right = right + wide(got_c[s, 1, i]) * factors[(sy, 1)]
            total = jnp.concatenate([left, right], axis=0)
            r = pl.multiple_of(y * 32, 32)
            new = joined[pl.ds(r, 32), :] * (total + 0.5) * low_inv[pl.ds(r, 32), :]
            if step + 1 < ITERS:
                joined[pl.ds(r, 32), :] = new
                ext[pl.ds(y + 16, 1), 16:48, :] = new.astype(BF16)[None]
            else:
                out_ref[pl.ds(y, 32, stride=32), :] = new

        def edges(i, _):
            finish(i, i, -1)
            finish(i + 17, i, 1)
            return 0

        lax.fori_loop(0, 15, edges, 0)
        finish(15, 0, 0)
        finish(16, 0, 0)
        if step + 1 < ITERS:
            send_ext()

    each(DIRS, lambda d: [c.wait_send() for c in corr_copies(d)])


def recv_ext(copy, s):
    copy((-s[0], -s[1])).wait_recv()


def recv_corr(copies, s):
    for c in copies((-s[0], -s[1])):
        c.wait_recv()


def body(fx_size, fy_size, estimate, images, psf, cover_lo, cover_len):
    vmem = pl.BlockSpec(memory_space=pltpu.VMEM)
    smem = pl.BlockSpec(memory_space=pltpu.SMEM)
    dma = pltpu.SemaphoreType.DMA
    out = pl.pallas_call(
        functools.partial(kernel, fx_size, fy_size),
        out_shape=jax.ShapeDtypeStruct((1024, 128), F32),
        in_specs=[vmem, vmem, vmem, smem, smem],
        out_specs=vmem,
        scratch_shapes=[
            pltpu.VMEM((64, 64, 128), BF16),
            pltpu.VMEM((1024, 128), F32),
            pltpu.VMEM((3, 1024, 128), BF16),
            pltpu.VMEM((6, 8, 128), F32),
            pltpu.VMEM((6, 16, 128), BF16),
            pltpu.VMEM((64 * 192, 128), F32),
            pltpu.VMEM((192 * 64, 128), F32),
            pltpu.VMEM((64, 64, 128), F32),
            pltpu.VMEM((64, 64, 128), I16),
            pltpu.VMEM((2, 32, 16, 128), I16),
            pltpu.VMEM((2, 15, 32, 128), I16),
            pltpu.VMEM((2, 2, 15, 16, 128), I16),
            pltpu.VMEM((8, 128), F32),
            pltpu.VMEM((8, 8, 128), F32),
            pltpu.VMEM((192, 128), BF16),
            pltpu.VMEM((6, 32, 128), BF16),
            pltpu.VMEM((6, 256, 128), BF16),
            pltpu.VMEM((6, 256, 128), BF16),
            pltpu.VMEM((6, 64, 128), BF16),
            pltpu.VMEM((64, 256), BF16),
            pltpu.VMEM((64, 256), BF16),
            pltpu.VMEM((1024, 128), F32),
            pltpu.VMEM((128, 128), F32),
            pltpu.VMEM((32, 128), F32),
            pltpu.VMEM((32, 128), F32),
            pltpu.VMEM((512, 128), F32),
            dma((8,)), dma((8,)), dma((8,)), dma((8,)),
            dma((8,)), dma((8,)), dma((5,)), dma((5,)),
        ],
        compiler_params=pltpu.CompilerParams(
            collective_id=0, has_side_effects=True, vmem_limit_bytes=60 << 20),
    )(
        estimate.reshape(1024, 128), images.reshape(3, 1024, 128), psf, cover_lo, cover_len)
    return out.reshape(32, 32, 128)


def solution(mesh):
    return jax.shard_map(
        functools.partial(body, mesh.shape["fx"], mesh.shape["fy"]),
        mesh=mesh,
        in_specs=(
            P("fx", "fy", None),
            P("view", "fx", "fy", None),
            P("view", None, None),
            P("view", None, None),
            P("view", None, None),
        ),
        out_specs=P("fx", "fy", None),
        check_vma=False,
    )
```

```python
import functools

import jax
import jax.numpy as jnp
from jax import lax
from jax.experimental import pallas as pl
from jax.experimental.pallas import tpu as pltpu
from jax.sharding import PartitionSpec as P

ITERS = 2
MESH = pl.DeviceIdType.MESH
BF16 = jnp.bfloat16
F32 = jnp.float32
I16 = jnp.int16
QMAX = 32000.0
PITCH_A = 200
PITCH_B = 72

DIRS = tuple((dy, dx) for dy in (-1, 0, 1) for dx in (-1, 0, 1) if dy or dx)
INDEX = {d: i for i, d in enumerate(DIRS)}
X_FACES = ((0, 1), (0, -1))
NOT_X_FACES = ((1, 0), (-1, 0), (1, 1), (1, -1), (-1, 1), (-1, -1))
SEND_ORDER = NOT_X_FACES[:2] + X_FACES + NOT_X_FACES[2:]

E_SRC_Y = {1: (33, 15), -1: (16, 15), 0: (16, 32)}
E_DST_Y = {-1: (1, 15), 1: (48, 15), 0: (16, 32)}
E_SRC_X = {1: (32, 16), -1: (16, 16), 0: (16, 32)}
E_DST_X = {-1: (0, 16), 1: (48, 16), 0: (16, 32)}
C_SRC_Y = {1: (48, 15), -1: (1, 15), 0: (16, 32)}
C_SRC_X = {1: (48, 16), -1: (0, 16), 0: (16, 32)}


def dot(a, b):
    return jnp.dot(a, b, preferred_element_type=F32)


def split(v):
    hi = v.astype(BF16)
    return hi, (v - hi.astype(F32)).astype(BF16)


def kernel(
    fx_size, fy_size,
    est_ref, img_ref, psf_ref, lo_ref, len_ref, out_ref,
    ext, joined, img2, kern, masks, wide_a, wide_b, corr, quant,
    got_x, got_y, got_c, scale, got_scale,
    fxt, fyt, fzt, bzt, byt, bxt, low_inv, mz, txs, tys, tpose, rows_u, rows_r, rows_v,
    e_send, e_recv, c_send, c_recv, s_send, s_recv, v_send, v_recv,
):
    g = lax.axis_index("view")
    bx = lax.axis_index("fx")
    by = lax.axis_index("fy")
    core = lax.rem(by, 2)
    own = g * 3
    oth = 3 - own

    def exists(d):
        dy, dx = d
        ok = jnp.bool_(True)
        if dy:
            ok = ok & (by + dy >= 0) & (by + dy < fy_size)
        if dx:
            ok = ok & (bx + dx >= 0) & (bx + dx < fx_size)
        return ok

    def peer(d):
        dy, dx = d
        cross = core if dy == 1 else (1 - core if dy == -1 else 0)
        return (g + cross - 2 * g * cross, bx + dx, by + dy)

    partner = (1 - g, bx, by)

    def ext_copy(d):
        s = (-d[0], -d[1])
        ys, ny = E_SRC_Y[d[0]]
        xs, nx = E_SRC_X[d[1]]
        yd, _ = E_DST_Y[s[0]]
        xd, _ = E_DST_X[s[1]]
        return pltpu.make_async_remote_copy(
            ext.at[pl.ds(ys, ny), pl.ds(xs, nx), :],
            ext.at[pl.ds(yd, ny), pl.ds(xd, nx), :],
            e_send.at[INDEX[d]], e_recv.at[INDEX[s]],
            device_id=peer(d), device_id_type=MESH)

    def landing(s):
        if s[0] == 0:
            return got_x.at[(s[1] + 1) // 2]
        if s[1] == 0:
            return got_y.at[(s[0] + 1) // 2]
        return got_c.at[(s[0] + 1) // 2, (s[1] + 1) // 2]

    def corr_copies(d):
        s = (-d[0], -d[1])
        ys, ny = C_SRC_Y[d[0]]
        xs, nx = C_SRC_X[d[1]]
        return (
            pltpu.make_async_remote_copy(
                scale, got_scale.at[INDEX[s]],
                s_send.at[INDEX[d]], s_recv.at[INDEX[s]],
                device_id=peer(d), device_id_type=MESH),
            pltpu.make_async_remote_copy(
                quant.at[pl.ds(ys, ny), pl.ds(xs, nx), :], landing(s),
                c_send.at[INDEX[d]], c_recv.at[INDEX[s]],
                device_id=peer(d), device_id_type=MESH),
        )

    def each(order, action):
        for d in order:
            @pl.when(exists(d))
            def _(d=d):
                action(d)

    def send_ext():
        each(SEND_ORDER, lambda d: ext_copy(d).start())

    kern[...] = jnp.zeros_like(kern)
    ext[...] = jnp.zeros_like(ext)

    barrier = pltpu.get_barrier_semaphore()
    count = jnp.int32(1)
    for d in DIRS:
        count = count + exists(d).astype(jnp.int32)
    pl.semaphore_signal(barrier, inc=1, device_id=partner, device_id_type=MESH)
    each(DIRS, lambda d: pl.semaphore_signal(
        barrier, inc=1, device_id=peer(d), device_id_type=MESH))


    def load_est(y, _):
        row = est_ref[pl.ds(y, 32, stride=32), :]
        joined[pl.ds(pl.multiple_of(y * 32, 32), 32), :] = row
        ext[pl.ds(y + 16, 1), 16:48, :] = row.astype(BF16)[None]
        return 0

    lax.fori_loop(0, 32, load_est, 0)

    lane = lax.broadcasted_iota(jnp.int32, (16, 128), 1)
    row16 = lax.broadcasted_iota(jnp.int32, (16, 128), 0)
    for k in range(3):
        taps = psf_ref[k]
        kern[pl.ds(own + k, 1), 0:3, 0:31] = (taps / jnp.sum(taps, axis=-1, keepdims=True))[None]
        low = jnp.zeros((16, 128), jnp.int32)
        top = jnp.zeros((16, 128), jnp.int32)
        for jy in range(3):
            for jx in range(3):
                px = bx + (jx - 1)
                py = by + (jy - 1)
                inside = (px >= 0) & (px < fx_size) & (py >= 0) & (py < fy_size)
                cx = jnp.clip(px, 0, fx_size - 1)
                cy = jnp.clip(py, 0, fy_size - 1)
                here = row16 == jy * 3 + jx
                start = lo_ref[k, cx, cy]
                span = len_ref[k, cx, cy] * inside.astype(jnp.int32)
                low = jnp.where(here, start, low)
                top = jnp.where(here, start + span, top)
        masks[pl.ds(own + k, 1)] = jnp.where(
            (lane >= low) & (lane < top), 1.0, 0.0).astype(BF16)[None]

    pl.semaphore_wait(barrier, count)

    send_ext()
    kern_copy = pltpu.make_async_remote_copy(
        kern.at[pl.ds(own, 3)], kern.at[pl.ds(own, 3)],
        v_send.at[3], v_recv.at[3], device_id=partner, device_id_type=MESH)
    mask_copy = pltpu.make_async_remote_copy(
        masks.at[pl.ds(own, 3)], masks.at[pl.ds(own, 3)],
        v_send.at[4], v_recv.at[4], device_id=partner, device_id_type=MESH)

    def img_copy(i):
        return pltpu.make_async_remote_copy(
            img_ref.at[i], img2.at[i], v_send.at[i], v_recv.at[i],
            device_id=partner, device_id_type=MESH)

    kern_copy.start()
    mask_copy.start()
    for i in range(3):
        img_copy(i).start()

    for d in DIRS:
        @pl.when(jnp.logical_not(exists(d)))
        def _(d=d):
            ref = landing(d)
            ref[...] = jnp.zeros(ref.shape, I16)
            got_scale[INDEX[d]] = jnp.zeros((8, 128), F32)

    kern_copy.wait()
    mask_copy.wait()

    zr = lax.broadcasted_iota(jnp.int32, (128, 128), 0)
    zc = lax.broadcasted_iota(jnp.int32, (128, 128), 1)
    near = (zc - zr <= 15) & (zr - zc <= 15)
    mz[...] = jnp.zeros_like(mz)

    def banded(row):
        return pltpu.roll(jnp.broadcast_to(row, (32, 128)), 1, 1, stride=1, stride_axis=0)

    lane32 = lax.broadcasted_iota(jnp.int32, (32, 128), 1)
    pos32 = lax.broadcasted_iota(jnp.int32, (32, 128), 0)

    def side_sums(row):
        taps = jnp.broadcast_to(row, (32, 128))
        before = jnp.sum(jnp.where(lane32 >= pos32 + 16, taps, 0.0), axis=1, keepdims=True)
        after = jnp.sum(jnp.where(lane32 <= pos32 - 17, taps, 0.0), axis=1, keepdims=True)
        middle = jnp.sum(
            jnp.where((lane32 < pos32 + 16) & (lane32 > pos32 - 17), taps, 0.0),
            axis=1, keepdims=True)
        return before, middle, after

    def tables(k, carry):
        sums_x, sums_y = carry
        rows = kern[k]
        near_x = rows[0:1].astype(BF16).astype(F32)
        near_y = rows[1:2].astype(BF16).astype(F32)
        gain_xy = (jnp.sum(near_x, axis=1, keepdims=True)
                   * jnp.sum(near_y, axis=1, keepdims=True))
        tx = banded(near_x)
        ty = banded(near_y)
        r = pl.multiple_of(k * 32, 32)
        fxt[pl.ds(r, 32), :] = tx.astype(BF16)
        fyt[k] = ty.astype(BF16)
        tpose[pl.ds(r, 32), :] = tx
        byt[k] = jnp.concatenate([ty, jnp.zeros((96, 128), F32)], axis=0).T[0:64, :].astype(BF16)
        tz = pltpu.roll(
            jnp.broadcast_to(rows[2:3] / gain_xy, (128, 128)), 113, 1, stride=1, stride_axis=0)
        tz = jnp.where(near, tz, 0.0)
        bh, bl = split(tz)
        bzt[k, 0:128] = bh
        bzt[k, 128:256] = bl
        fh, fl = split(tz.T)
        fzt[k, 0:128] = fh
        fzt[k, 128:256] = fl
        m = masks[k]
        mz[pl.ds(pl.multiple_of(k * 16, 16), 16), :] = dot(
            jnp.concatenate([m, m], axis=1), bzt[k]) * gain_xy
        part = lane32 - k * 16
        mine = (part >= 0) & (part < 9)
        px = lax.rem(part + 96, 3)
        py = (part + 96) // 3 - 32
        for j, col in enumerate(side_sums(rows[0:1])):
            sums_x = jnp.where(mine & (px == j), col, sums_x)
        for j, col in enumerate(side_sums(rows[1:2])):
            sums_y = jnp.where(mine & (py == j), col, sums_y)
        return sums_x, sums_y

    zero = jnp.zeros((32, 128), F32)
    sums_x, sums_y = lax.fori_loop(0, 6, tables, (zero, zero))
    txs[...] = sums_x
    tys[...] = sums_y
    bxt[:, 0:128] = tpose[0:128, :].T[0:64].astype(BF16)
    bxt[:, 128:256] = tpose[128:256, :].T[0:64].astype(BF16)

    def weigh(q, _):
        parts = []
        for j in range(8):
            parts.append(txs[...] * tys[pl.ds(q * 8 + j, 1), :])
        w = jnp.dot(jnp.concatenate(parts, axis=0), mz[...],
                    preferred_element_type=F32, precision=lax.Precision.HIGHEST)
        low_inv[pl.ds(pl.multiple_of(q * 256, 256), 256), :] = 1.0 / (w + 0.5)
        return 0

    lax.fori_loop(0, 4, weigh, 0)

    def view_step(k, images):
        covered = masks[k, 4:5, :].astype(F32) > 0.5
        ty = fyt[k][:, 0:64]
        for p in range(16):
            cols = jnp.concatenate(
                [wide_a[pl.ds(k * 32 + p * 2 + j, 64, stride=PITCH_A), :].astype(BF16)
                 for j in range(2)], axis=1)
            out = dot(ty, cols).astype(BF16)
            rows_u[p * 64:p * 64 + 32, :] = out[:, 0:128]
            rows_u[p * 64 + 32:p * 64 + 64, :] = out[:, 128:256]
        for c in range(4):
            part = slice(c * 256, c * 256 + 256)
            u = rows_u[part, :]
            f = dot(jnp.concatenate([u, u], axis=1), fzt[k])
            pic = jnp.where(covered, images[part, :].astype(F32), 0.0)
            rows_r[part, :] = (pic / f).astype(BF16)
        for c in range(4):
            part = slice(c * 256, c * 256 + 256)
            r = rows_r[part, :]
            rows_v[part, :] = dot(jnp.concatenate([r, r], axis=1), bzt[k]).astype(BF16)
        back = byt[k][:, 0:32]
        for p in range(16):
            cols = jnp.concatenate(
                [rows_v[p * 64 + j * 32:p * 64 + j * 32 + 32, :] for j in range(2)], axis=1)
            out = dot(back, cols)
            for j in range(2):
                r = pl.multiple_of((k * 32 + p * 2 + j) * PITCH_B, 8)
                wide_b[pl.ds(r, 64), :] = out[:, j * 128:j * 128 + 128]

    for step in range(ITERS):
        def pass_x(p, _):
            cols = jnp.concatenate([ext[p * 2], ext[p * 2 + 1]], axis=1)
            out = dot(fxt[:, 0:64], cols)
            for j in range(2):
                r = pl.multiple_of((p * 2 + j) * PITCH_A, 8)
                wide_a[pl.ds(r, 192), :] = out[:, j * 128:j * 128 + 128]
            return 0

        each(X_FACES, lambda d: recv_ext(ext_copy, d))
        lax.fori_loop(8, 24, pass_x, 0, unroll=4)
        each(NOT_X_FACES, lambda d: recv_ext(ext_copy, d))
        lax.fori_loop(0, 8, pass_x, 0, unroll=4)
        lax.fori_loop(24, 32, pass_x, 0, unroll=4)

        def own_views(n, _):
            view_step(own + n, img_ref.at[n])
            return 0

        lax.fori_loop(0, 3, own_views, 0)

        if step == 0:
            for i in range(3):
                img_copy(i).wait()

        def other_views(n, _):
            view_step(oth + n, img2.at[n])
            return 0

        lax.fori_loop(0, 3, other_views, 0)

        def back_x(p, peak):
            pair = [wide_b[pl.ds(p * 2 + j, 192, stride=PITCH_B), :] for j in range(2)]
            hi, lo = split(jnp.concatenate(pair, axis=1))
            th = bxt[:, 0:192]
            out = dot(th, hi) + dot(th, lo)
            for j in range(2):
                part = out[:, j * 128:j * 128 + 128]
                corr[p * 2 + j] = part
                peak = jnp.maximum(peak, part)
            return peak

        peak = lax.fori_loop(0, 32, back_x, jnp.zeros((64, 128), F32), unroll=4)
        peak = jnp.max(jnp.max(peak, axis=0, keepdims=True), axis=1, keepdims=True)
        peak = jnp.maximum(peak, 1e-30)

        if step > 0:
            each(DIRS, lambda d: [c.wait_send() for c in corr_copies(d)])
        scale[...] = jnp.broadcast_to(peak * (1.0 / QMAX), (8, 128))
        gain = jnp.broadcast_to(QMAX / peak, (64, 128))

        def code(y, _):
            quant[y] = jnp.round(corr[y] * gain).astype(jnp.int32).astype(I16)
            return 0

        lax.fori_loop(0, 64, code, 0, unroll=4)
        each(SEND_ORDER, lambda d: [c.start() for c in corr_copies(d)])
        each(DIRS, lambda d: ext_copy(d).wait_send())
        each(DIRS, lambda d: recv_corr(corr_copies, d))

        factors = {d: jnp.broadcast_to(got_scale[INDEX[d], 0:1, :], (16, 128)) for d in DIRS}

        def wide(ref):
            return ref.astype(jnp.int32).astype(F32)

        def finish(y, i, sy):
            left = corr[y + 16, 16:32, :] + wide(got_x[0, y]) * factors[(0, -1)]
            right = corr[y + 16, 32:48, :] + wide(got_x[1, y]) * factors[(0, 1)]
            if sy:
                s = (sy + 1) // 2
                left = left + wide(got_y[s, i, 0:16]) * factors[(sy, 0)]
                left = left + wide(got_c[s, 0, i]) * factors[(sy, -1)]
                right = right + wide(got_y[s, i, 16:32]) * factors[(sy, 0)]
                right = right + wide(got_c[s, 1, i]) * factors[(sy, 1)]
            total = jnp.concatenate([left, right], axis=0)
            r = pl.multiple_of(y * 32, 32)
            new = joined[pl.ds(r, 32), :] * (total + 0.5) * low_inv[pl.ds(r, 32), :]
            if step + 1 < ITERS:
                joined[pl.ds(r, 32), :] = new
                ext[pl.ds(y + 16, 1), 16:48, :] = new.astype(BF16)[None]
            else:
                out_ref[pl.ds(y, 32, stride=32), :] = new

        def edges(i, _):
            finish(i, i, -1)
            finish(i + 17, i, 1)
            return 0

        lax.fori_loop(0, 15, edges, 0)
        finish(15, 0, 0)
        finish(16, 0, 0)
        if step + 1 < ITERS:
            send_ext()

    each(DIRS, lambda d: [c.wait_send() for c in corr_copies(d)])


def recv_ext(copy, s):
    copy((-s[0], -s[1])).wait_recv()


def recv_corr(copies, s):
    for c in copies((-s[0], -s[1])):
        c.wait_recv()


def body(fx_size, fy_size, estimate, images, psf, cover_lo, cover_len):
    vmem = pl.BlockSpec(memory_space=pltpu.VMEM)
    smem = pl.BlockSpec(memory_space=pltpu.SMEM)
    dma = pltpu.SemaphoreType.DMA
    out = pl.pallas_call(
        functools.partial(kernel, fx_size, fy_size),
        out_shape=jax.ShapeDtypeStruct((1024, 128), F32),
        in_specs=[vmem, vmem, vmem, smem, smem],
        out_specs=vmem,
        scratch_shapes=[
            pltpu.VMEM((64, 64, 128), BF16),
            pltpu.VMEM((1024, 128), F32),
            pltpu.VMEM((3, 1024, 128), BF16),
            pltpu.VMEM((6, 8, 128), F32),
            pltpu.VMEM((6, 16, 128), BF16),
            pltpu.VMEM((64 * PITCH_A, 128), F32),
            pltpu.VMEM((192 * PITCH_B, 128), F32),
            pltpu.VMEM((64, 64, 128), F32),
            pltpu.VMEM((64, 64, 128), I16),
            pltpu.VMEM((2, 32, 16, 128), I16),
            pltpu.VMEM((2, 15, 32, 128), I16),
            pltpu.VMEM((2, 2, 15, 16, 128), I16),
            pltpu.VMEM((8, 128), F32),
            pltpu.VMEM((8, 8, 128), F32),
            pltpu.VMEM((192, 128), BF16),
            pltpu.VMEM((6, 32, 128), BF16),
            pltpu.VMEM((6, 256, 128), BF16),
            pltpu.VMEM((6, 256, 128), BF16),
            pltpu.VMEM((6, 64, 128), BF16),
            pltpu.VMEM((64, 256), BF16),
            pltpu.VMEM((1024, 128), F32),
            pltpu.VMEM((128, 128), F32),
            pltpu.VMEM((32, 128), F32),
            pltpu.VMEM((32, 128), F32),
            pltpu.VMEM((256, 128), F32),
            pltpu.VMEM((1024, 128), BF16),
            pltpu.VMEM((1024, 128), BF16),
            pltpu.VMEM((1024, 128), BF16),
            dma((8,)), dma((8,)), dma((8,)), dma((8,)),
            dma((8,)), dma((8,)), dma((5,)), dma((5,)),
        ],
        compiler_params=pltpu.CompilerParams(
            collective_id=0, has_side_effects=True, vmem_limit_bytes=60 << 20),
    )(
        estimate.reshape(1024, 128), images.reshape(3, 1024, 128), psf, cover_lo, cover_len)
    return out.reshape(32, 32, 128)


def solution(mesh):
    return jax.shard_map(
        functools.partial(body, mesh.shape["fx"], mesh.shape["fy"]),
        mesh=mesh,
        in_specs=(
            P("fx", "fy", None),
            P("view", "fx", "fy", None),
            P("view", None, None),
            P("view", None, None),
            P("view", None, None),
        ),
        out_specs=P("fx", "fy", None),
        check_vma=False,
    )
```

```python
import functools

import jax
import jax.numpy as jnp
from jax import lax
from jax.experimental import pallas as pl
from jax.experimental.pallas import tpu as pltpu
from jax.sharding import PartitionSpec as P

ITERS = 2
MESH = pl.DeviceIdType.MESH
BF16 = jnp.bfloat16
F32 = jnp.float32
I16 = jnp.int16
QMAX = 32000.0
PITCH_A = 200
PITCH_B = 72

DIRS = tuple((dy, dx) for dy in (-1, 0, 1) for dx in (-1, 0, 1) if dy or dx)
INDEX = {d: i for i, d in enumerate(DIRS)}
X_FACES = ((0, 1), (0, -1))
NOT_X_FACES = ((1, 0), (-1, 0), (1, 1), (1, -1), (-1, 1), (-1, -1))
SEND_ORDER = NOT_X_FACES[:2] + X_FACES + NOT_X_FACES[2:]

E_SRC_Y = {1: (33, 15), -1: (16, 15), 0: (16, 32)}
E_DST_Y = {-1: (1, 15), 1: (48, 15), 0: (16, 32)}
E_SRC_X = {1: (32, 16), -1: (16, 16), 0: (16, 32)}
E_DST_X = {-1: (0, 16), 1: (48, 16), 0: (16, 32)}
C_SRC_Y = {1: (48, 15), -1: (1, 15), 0: (16, 32)}
C_SRC_X = {1: (48, 16), -1: (0, 16), 0: (16, 32)}


def dot(a, b):
    return jnp.dot(a, b, preferred_element_type=F32)


def split(v):
    hi = v.astype(BF16)
    return hi, (v - hi.astype(F32)).astype(BF16)


def kernel(
    fx_size, fy_size,
    est_any, img_any, psf_ref, lo_ref, len_ref, out_any,
    block, img_ref, img_pack, img_got,
    ext, joined, img2, kern, masks, wide_a, wide_b, corr, quant,
    got_x, got_y, got_c, scale, got_scale,
    fxt, fyt, fzt, bzt, byt, bxt, low_inv, mz, txs, tys, tpose, rows_u, rows_r, rows_v,
    e_send, e_recv, c_send, c_recv, s_send, s_recv, v_send, v_recv, own_sem,
):
    g = lax.axis_index("view")
    bx = lax.axis_index("fx")
    by = lax.axis_index("fy")
    core = lax.rem(by, 2)
    own = g * 3
    oth = 3 - own

    def exists(d):
        dy, dx = d
        ok = jnp.bool_(True)
        if dy:
            ok = ok & (by + dy >= 0) & (by + dy < fy_size)
        if dx:
            ok = ok & (bx + dx >= 0) & (bx + dx < fx_size)
        return ok

    def peer(d):
        dy, dx = d
        cross = core if dy == 1 else (1 - core if dy == -1 else 0)
        return (g + cross - 2 * g * cross, bx + dx, by + dy)

    partner = (1 - g, bx, by)

    def ext_copy(d):
        s = (-d[0], -d[1])
        ys, ny = E_SRC_Y[d[0]]
        xs, nx = E_SRC_X[d[1]]
        yd, _ = E_DST_Y[s[0]]
        xd, _ = E_DST_X[s[1]]
        return pltpu.make_async_remote_copy(
            ext.at[pl.ds(ys, ny), pl.ds(xs, nx), :],
            ext.at[pl.ds(yd, ny), pl.ds(xd, nx), :],
            e_send.at[INDEX[d]], e_recv.at[INDEX[s]],
            device_id=peer(d), device_id_type=MESH)

    def landing(s):
        if s[0] == 0:
            return got_x.at[(s[1] + 1) // 2]
        if s[1] == 0:
            return got_y.at[(s[0] + 1) // 2]
        return got_c.at[(s[0] + 1) // 2, (s[1] + 1) // 2]

    def corr_copies(d):
        s = (-d[0], -d[1])
        ys, ny = C_SRC_Y[d[0]]
        xs, nx = C_SRC_X[d[1]]
        return (
            pltpu.make_async_remote_copy(
                scale.at[0 if d[0] else 1], got_scale.at[INDEX[s]],
                s_send.at[INDEX[d]], s_recv.at[INDEX[s]],
                device_id=peer(d), device_id_type=MESH),
            pltpu.make_async_remote_copy(
                quant.at[pl.ds(ys, ny), pl.ds(xs, nx), :], landing(s),
                c_send.at[INDEX[d]], c_recv.at[INDEX[s]],
                device_id=peer(d), device_id_type=MESH),
        )

    def each(order, action):
        for d in order:
            @pl.when(exists(d))
            def _(d=d):
                action(d)

    def send_ext():
        each(SEND_ORDER, lambda d: ext_copy(d).start())

    est_copy = pltpu.make_async_copy(est_any, block.at[:, 0:32, :], own_sem.at[0])
    est_copy.start()
    own_images = pltpu.make_async_copy(img_any, img_ref, own_sem.at[1])
    own_images.start()
    kern[...] = jnp.zeros_like(kern)
    ext[...] = jnp.zeros_like(ext)

    barrier = pltpu.get_barrier_semaphore()
    count = jnp.int32(1)
    for d in DIRS:
        count = count + exists(d).astype(jnp.int32)
    pl.semaphore_signal(barrier, inc=1, device_id=partner, device_id_type=MESH)
    each(DIRS, lambda d: pl.semaphore_signal(
        barrier, inc=1, device_id=peer(d), device_id_type=MESH))


    flat = block.reshape(32 * 40, 128)
    est_copy.wait()

    def load_est(y, _):
        row = flat[pl.ds(y, 32, stride=40), :]
        joined[pl.ds(pl.multiple_of(y * 32, 32), 32), :] = row
        ext[pl.ds(y + 16, 1), 16:48, :] = row.astype(BF16)[None]
        return 0

    lax.fori_loop(0, 32, load_est, 0, unroll=4)

    lane = lax.broadcasted_iota(jnp.int32, (16, 128), 1)
    row16 = lax.broadcasted_iota(jnp.int32, (16, 128), 0)
    for k in range(3):
        taps = psf_ref[k]
        kern[pl.ds(own + k, 1), 0:3, 0:31] = (taps / jnp.sum(taps, axis=-1, keepdims=True))[None]
        low = jnp.zeros((16, 128), jnp.int32)
        top = jnp.zeros((16, 128), jnp.int32)
        for jy in range(3):
            for jx in range(3):
                px = bx + (jx - 1)
                py = by + (jy - 1)
                inside = (px >= 0) & (px < fx_size) & (py >= 0) & (py < fy_size)
                cx = jnp.clip(px, 0, fx_size - 1)
                cy = jnp.clip(py, 0, fy_size - 1)
                here = row16 == jy * 3 + jx
                start = lo_ref[k, cx, cy]
                span = len_ref[k, cx, cy] * inside.astype(jnp.int32)
                low = jnp.where(here, start, low)
                top = jnp.where(here, start + span, top)
        masks[pl.ds(own + k, 1)] = jnp.where(
            (lane >= low) & (lane < top), 1.0, 0.0).astype(BF16)[None]

    pl.semaphore_wait(barrier, count)

    send_ext()
    kern_copy = pltpu.make_async_remote_copy(
        kern.at[pl.ds(own, 3)], kern.at[pl.ds(own, 3)],
        v_send.at[3], v_recv.at[3], device_id=partner, device_id_type=MESH)
    mask_copy = pltpu.make_async_remote_copy(
        masks.at[pl.ds(own, 3)], masks.at[pl.ds(own, 3)],
        v_send.at[4], v_recv.at[4], device_id=partner, device_id_type=MESH)

    def img_copy(i):
        return pltpu.make_async_remote_copy(
            img_pack.at[i], img_got.at[i], v_send.at[i], v_recv.at[i],
            device_id=partner, device_id_type=MESH)

    kern_copy.start()
    mask_copy.start()

    low_half = lax.broadcasted_iota(jnp.int32, (64, 128), 1) < 64
    own_images.wait()
    for i in range(3):
        kept = jnp.broadcast_to(masks[own + i, 4:5, :].astype(F32), (64, 128)) > 0.5

        def fold(c, _, i=i, kept=kept):
            r = pl.multiple_of(c * 64, 64)
            first = jnp.where(kept, img_ref[i, pl.ds(r, 64), :].astype(F32), 0.0)
            second = jnp.where(kept, img_ref[i, pl.ds(r + 512, 64), :].astype(F32), 0.0)
            stay = jnp.where(low_half, first, second)
            move = jnp.where(low_half, second, first)
            img_pack[i, pl.ds(r, 64), :] = (stay + pltpu.roll(move, 64, 1)).astype(BF16)
            return 0

        lax.fori_loop(0, 8, fold, 0, unroll=2)
        img_copy(i).start()

    for d in DIRS:
        @pl.when(jnp.logical_not(exists(d)))
        def _(d=d):
            ref = landing(d)
            ref[...] = jnp.zeros(ref.shape, I16)
            got_scale[INDEX[d]] = jnp.zeros((8, 128), F32)

    kern_copy.wait()
    mask_copy.wait()

    zr = lax.broadcasted_iota(jnp.int32, (128, 128), 0)
    zc = lax.broadcasted_iota(jnp.int32, (128, 128), 1)
    near = (zc - zr <= 15) & (zr - zc <= 15)
    mz[...] = jnp.zeros_like(mz)

    def banded(row):
        return pltpu.roll(jnp.broadcast_to(row, (32, 128)), 1, 1, stride=1, stride_axis=0)

    lane32 = lax.broadcasted_iota(jnp.int32, (32, 128), 1)
    pos32 = lax.broadcasted_iota(jnp.int32, (32, 128), 0)

    def side_sums(row):
        taps = jnp.broadcast_to(row, (32, 128))
        before = jnp.sum(jnp.where(lane32 >= pos32 + 16, taps, 0.0), axis=1, keepdims=True)
        after = jnp.sum(jnp.where(lane32 <= pos32 - 17, taps, 0.0), axis=1, keepdims=True)
        middle = jnp.sum(
            jnp.where((lane32 < pos32 + 16) & (lane32 > pos32 - 17), taps, 0.0),
            axis=1, keepdims=True)
        return before, middle, after

    def tables(k, carry):
        sums_x, sums_y = carry
        rows = kern[k]
        near_x = rows[0:1].astype(BF16).astype(F32)
        near_y = rows[1:2].astype(BF16).astype(F32)
        near_z = rows[2:3].astype(BF16).astype(F32)
        gain = (jnp.sum(near_x, axis=1, keepdims=True)
                * jnp.sum(near_y, axis=1, keepdims=True)
                * jnp.sum(near_z, axis=1, keepdims=True))
        tx = banded(near_x)
        ty = banded(near_y)
        r = pl.multiple_of(k * 32, 32)
        fxt[pl.ds(r, 32), :] = tx.astype(BF16)
        fyt[k] = ty.astype(BF16)
        tpose[pl.ds(r, 32), :] = tx
        byt[k] = jnp.concatenate([ty, jnp.zeros((96, 128), F32)], axis=0).T[0:64, :].astype(BF16)
        tz = pltpu.roll(jnp.broadcast_to(near_z, (128, 128)), 113, 1, stride=1, stride_axis=0)
        tz = jnp.where(near, tz, 0.0)
        bzt[k] = tz.astype(BF16)
        fzt[k] = tz.T.astype(BF16)
        m = masks[k]
        mz[pl.ds(pl.multiple_of(k * 16, 16), 16), :] = dot(
            m, bzt[k]) / gain
        part = lane32 - k * 16
        mine = (part >= 0) & (part < 9)
        px = lax.rem(part + 96, 3)
        py = (part + 96) // 3 - 32
        for j, col in enumerate(side_sums(near_x)):
            sums_x = jnp.where(mine & (px == j), col, sums_x)
        for j, col in enumerate(side_sums(near_y)):
            sums_y = jnp.where(mine & (py == j), col, sums_y)
        return sums_x, sums_y

    zero = jnp.zeros((32, 128), F32)
    sums_x, sums_y = lax.fori_loop(0, 6, tables, (zero, zero))
    txs[...] = sums_x
    tys[...] = sums_y
    bxt[:, 0:128] = tpose[0:128, :].T[0:64].astype(BF16)
    bxt[:, 128:256] = tpose[128:256, :].T[0:64].astype(BF16)

    def weigh(q, _):
        parts = []
        for j in range(8):
            parts.append(txs[...] * tys[pl.ds(q * 8 + j, 1), :])
        w = jnp.dot(jnp.concatenate(parts, axis=0), mz[...],
                    preferred_element_type=F32, precision=lax.Precision.HIGHEST)
        low_inv[pl.ds(pl.multiple_of(q * 256, 256), 256), :] = 1.0 / (w + 0.5)
        return 0

    lax.fori_loop(0, 4, weigh, 0)

    def view_step(k, images):
        covered = masks[k, 4:5, :].astype(F32) > 0.5
        ty = fyt[k][:, 0:64]
        for p in range(16):
            cols = jnp.concatenate(
                [wide_a[pl.ds(k * 32 + p * 2 + j, 64, stride=PITCH_A), :].astype(BF16)
                 for j in range(2)], axis=1)
            out = dot(ty, cols).astype(BF16)
            rows_u[p * 64:p * 64 + 32, :] = out[:, 0:128]
            rows_u[p * 64 + 32:p * 64 + 64, :] = out[:, 128:256]
        for c in range(4):
            part = slice(c * 256, c * 256 + 256)
            u = rows_u[part, :]
            f = dot(u, fzt[k])
            pic = jnp.where(covered, images[part, :].astype(F32), 0.0)
            rows_r[part, :] = (pic / f).astype(BF16)
        for c in range(4):
            part = slice(c * 256, c * 256 + 256)
            r = rows_r[part, :]
            rows_v[part, :] = dot(r, bzt[k]).astype(BF16)
        back = byt[k][:, 0:32]
        for p in range(16):
            cols = jnp.concatenate(
                [rows_v[p * 64 + j * 32:p * 64 + j * 32 + 32, :] for j in range(2)], axis=1)
            out = dot(back, cols)
            for j in range(2):
                r = pl.multiple_of((k * 32 + p * 2 + j) * PITCH_B, 8)
                wide_b[pl.ds(r, 64), :] = out[:, j * 128:j * 128 + 128]

    for step in range(ITERS):
        def pass_x(p, _):
            cols = jnp.concatenate([ext[p * 2], ext[p * 2 + 1]], axis=1)
            out = dot(fxt[:, 0:64], cols)
            for j in range(2):
                r = pl.multiple_of((p * 2 + j) * PITCH_A, 8)
                wide_a[pl.ds(r, 192), :] = out[:, j * 128:j * 128 + 128]
            return 0

        each(X_FACES, lambda d: recv_ext(ext_copy, d))
        lax.fori_loop(8, 24, pass_x, 0, unroll=8)
        each(NOT_X_FACES, lambda d: recv_ext(ext_copy, d))
        lax.fori_loop(0, 8, pass_x, 0, unroll=8)
        lax.fori_loop(24, 32, pass_x, 0, unroll=8)

        def own_views(n, _):
            view_step(own + n, img_ref.at[n])
            return 0

        lax.fori_loop(0, 3, own_views, 0)

        if step == 0:
            for i in range(3):
                img_copy(i).wait()

                def unfold(c, _, i=i):
                    r = pl.multiple_of(c * 64, 64)
                    stay = img_got[i, pl.ds(r, 64), :].astype(F32)
                    move = pltpu.roll(stay, 64, 1)
                    img2[i, pl.ds(r, 64), :] = jnp.where(low_half, stay, move).astype(BF16)
                    img2[i, pl.ds(r + 512, 64), :] = jnp.where(low_half, move, stay).astype(BF16)
                    return 0

                lax.fori_loop(0, 8, unfold, 0, unroll=2)

        def other_views(n, _):
            view_step(oth + n, img2.at[n])
            return 0

        lax.fori_loop(0, 3, other_views, 0)

        def back_x(p, peak):
            pair = [wide_b[pl.ds(p * 2 + j, 192, stride=PITCH_B), :] for j in range(2)]
            hi, lo = split(jnp.concatenate(pair, axis=1))
            th = bxt[:, 0:192]
            out = dot(th, hi) + dot(th, lo)
            for j in range(2):
                part = out[:, j * 128:j * 128 + 128]
                corr[p * 2 + j] = part
                peak = jnp.maximum(peak, part)
            return peak

        def gain_of(peak, slot):
            peak = jnp.max(jnp.max(peak, axis=0, keepdims=True), axis=1, keepdims=True)
            peak = jnp.maximum(peak, 1e-30)
            scale[slot] = jnp.broadcast_to(peak * (1.0 / QMAX), (8, 128))
            return jnp.broadcast_to(QMAX / peak, (16, 128))

        def put(y, x, gain):
            quant[y, x:x + 16, :] = jnp.round(
                corr[y, x:x + 16, :] * gain).astype(jnp.int32).astype(I16)

        if step > 0:
            each(DIRS, lambda d: [c.wait_send() for c in corr_copies(d)])
        zeros = jnp.zeros((64, 128), F32)
        peak = lax.fori_loop(0, 8, back_x, zeros, unroll=4)
        peak = lax.fori_loop(24, 32, back_x, peak, unroll=4)
        outer = gain_of(peak, 0)

        def code_outer(y, _):
            for x in (0, 16, 32, 48):
                put(y, x, outer)
                put(y + 48, x, outer)
            return 0

        lax.fori_loop(0, 16, code_outer, 0, unroll=2)
        each(NOT_X_FACES, lambda d: [c.start() for c in corr_copies(d)])

        peak = lax.fori_loop(8, 24, back_x, zeros, unroll=4)
        inner = gain_of(peak, 1)

        def code_inner(y, _):
            put(y, 0, inner)
            put(y, 48, inner)
            return 0

        lax.fori_loop(16, 48, code_inner, 0, unroll=4)
        each(X_FACES, lambda d: [c.start() for c in corr_copies(d)])
        each(DIRS, lambda d: ext_copy(d).wait_send())
        each(DIRS, lambda d: recv_corr(corr_copies, d))

        factors = {d: jnp.broadcast_to(got_scale[INDEX[d], 0:1, :], (16, 128)) for d in DIRS}

        def wide(ref):
            return ref.astype(jnp.int32).astype(F32)

        def finish(y, i, sy):
            left = corr[y + 16, 16:32, :] + wide(got_x[0, y]) * factors[(0, -1)]
            right = corr[y + 16, 32:48, :] + wide(got_x[1, y]) * factors[(0, 1)]
            if sy:
                s = (sy + 1) // 2
                left = left + wide(got_y[s, i, 0:16]) * factors[(sy, 0)]
                left = left + wide(got_c[s, 0, i]) * factors[(sy, -1)]
                right = right + wide(got_y[s, i, 16:32]) * factors[(sy, 0)]
                right = right + wide(got_c[s, 1, i]) * factors[(sy, 1)]
            total = jnp.concatenate([left, right], axis=0)
            r = pl.multiple_of(y * 32, 32)
            new = joined[pl.ds(r, 32), :] * (total + 0.5) * low_inv[pl.ds(r, 32), :]
            if step + 1 < ITERS:
                joined[pl.ds(r, 32), :] = new
                ext[pl.ds(y + 16, 1), 16:48, :] = new.astype(BF16)[None]
            else:
                flat[pl.ds(y, 32, stride=40), :] = new

        def edges(i, _):
            finish(i, i, -1)
            finish(i + 17, i, 1)
            return 0

        lax.fori_loop(0, 15, edges, 0)
        finish(15, 0, 0)
        finish(16, 0, 0)
        if step + 1 < ITERS:
            send_ext()

    out_copy = pltpu.make_async_copy(block.at[:, 0:32, :], out_any, own_sem.at[2])
    out_copy.start()
    each(DIRS, lambda d: [c.wait_send() for c in corr_copies(d)])
    out_copy.wait()


def recv_ext(copy, s):
    copy((-s[0], -s[1])).wait_recv()


def recv_corr(copies, s):
    for c in copies((-s[0], -s[1])):
        c.wait_recv()


def body(fx_size, fy_size, estimate, images, psf, cover_lo, cover_len):
    vmem = pl.BlockSpec(memory_space=pltpu.VMEM)
    smem = pl.BlockSpec(memory_space=pltpu.SMEM)
    anywhere = pl.BlockSpec(memory_space=pl.ANY)
    dma = pltpu.SemaphoreType.DMA
    out = pl.pallas_call(
        functools.partial(kernel, fx_size, fy_size),
        out_shape=jax.ShapeDtypeStruct((32, 32, 128), F32),
        in_specs=[anywhere, anywhere, vmem, smem, smem],
        out_specs=anywhere,
        scratch_shapes=[
            pltpu.VMEM((32, 40, 128), F32),
            pltpu.VMEM((3, 1024, 128), BF16),
            pltpu.VMEM((3, 512, 128), BF16),
            pltpu.VMEM((3, 512, 128), BF16),
            pltpu.VMEM((64, 64, 128), BF16),
            pltpu.VMEM((1024, 128), F32),
            pltpu.VMEM((3, 1024, 128), BF16),
            pltpu.VMEM((6, 8, 128), F32),
            pltpu.VMEM((6, 16, 128), BF16),
            pltpu.VMEM((64 * PITCH_A, 128), F32),
            pltpu.VMEM((192 * PITCH_B, 128), F32),
            pltpu.VMEM((64, 64, 128), F32),
            pltpu.VMEM((64, 64, 128), I16),
            pltpu.VMEM((2, 32, 16, 128), I16),
            pltpu.VMEM((2, 15, 32, 128), I16),
            pltpu.VMEM((2, 2, 15, 16, 128), I16),
            pltpu.VMEM((2, 8, 128), F32),
            pltpu.VMEM((8, 8, 128), F32),
            pltpu.VMEM((192, 128), BF16),
            pltpu.VMEM((6, 32, 128), BF16),
            pltpu.VMEM((6, 128, 128), BF16),
            pltpu.VMEM((6, 128, 128), BF16),
            pltpu.VMEM((6, 64, 128), BF16),
            pltpu.VMEM((64, 256), BF16),
            pltpu.VMEM((1024, 128), F32),
            pltpu.VMEM((128, 128), F32),
            pltpu.VMEM((32, 128), F32),
            pltpu.VMEM((32, 128), F32),
            pltpu.VMEM((256, 128), F32),
            pltpu.VMEM((1024, 128), BF16),
            pltpu.VMEM((1024, 128), BF16),
            pltpu.VMEM((1024, 128), BF16),
            dma((8,)), dma((8,)), dma((8,)), dma((8,)),
            dma((8,)), dma((8,)), dma((5,)), dma((5,)), dma((3,)),
        ],
        compiler_params=pltpu.CompilerParams(
            collective_id=0, has_side_effects=True, vmem_limit_bytes=60 << 20),
    )(
        estimate, images.reshape(3, 1024, 128), psf, cover_lo, cover_len)
    return out


def solution(mesh):
    return jax.shard_map(
        functools.partial(body, mesh.shape["fx"], mesh.shape["fy"]),
        mesh=mesh,
        in_specs=(
            P("fx", "fy", None),
            P("view", "fx", "fy", None),
            P("view", None, None),
            P("view", None, None),
            P("view", None, None),
        ),
        out_specs=P("fx", "fy", None),
        check_vma=False,
    )
```

```python
import functools

import jax
import jax.numpy as jnp
from jax import lax
from jax.experimental import pallas as pl
from jax.experimental.pallas import tpu as pltpu
from jax.sharding import PartitionSpec as P

ITERS = 2
MESH = pl.DeviceIdType.MESH
BF16 = jnp.bfloat16
F32 = jnp.float32
I16 = jnp.int16
QMAX = 32000.0
PITCH_A = 196
PITCH_B = 68

DIRS = tuple((dy, dx) for dy in (-1, 0, 1) for dx in (-1, 0, 1) if dy or dx)
INDEX = {d: i for i, d in enumerate(DIRS)}
X_FACES = ((0, 1), (0, -1))
NOT_X_FACES = ((1, 0), (-1, 0), (1, 1), (1, -1), (-1, 1), (-1, -1))
Y_FACES = NOT_X_FACES[:2]
CORNERS = NOT_X_FACES[2:]

E_SRC_Y = {1: (33, 15), -1: (16, 15), 0: (16, 32)}
E_DST_Y = {-1: (1, 15), 1: (48, 15), 0: (16, 32)}
E_SRC_X = {1: (32, 16), -1: (16, 16), 0: (16, 32)}
E_DST_X = {-1: (0, 16), 1: (48, 16), 0: (16, 32)}
C_SRC_Y = {1: (48, 15), -1: (1, 15), 0: (16, 32)}
C_SRC_X = {1: (48, 16), -1: (0, 16), 0: (16, 32)}


def dot(a, b):
    return jnp.dot(a, b, preferred_element_type=F32)


def split(v):
    hi = v.astype(BF16)
    return hi, (v - hi.astype(F32)).astype(BF16)


def kernel(
    fx_size, fy_size,
    est_any, img_any, psf_ref, lo_ref, len_ref, out_ref,
    block, img_ref, img_pack, img_got,
    ext, joined, img2, kern, masks, wide_a, wide_b, corr, quant,
    got_x, got_y, got_c, scale, got_scale,
    fxt, fyt, fzt, bzt, byt, bxt, low_inv, mz, txs, tys, tpose, rows_u, rows_r, rows_v,
    e_send, e_recv, c_send, c_recv, s_send, s_recv, v_send, v_recv, own_sem,
):
    g = lax.axis_index("view")
    bx = lax.axis_index("fx")
    by = lax.axis_index("fy")
    core = lax.rem(by, 2)
    own = g * 3
    oth = 3 - own

    def exists(d):
        dy, dx = d
        ok = jnp.bool_(True)
        if dy:
            ok = ok & (by + dy >= 0) & (by + dy < fy_size)
        if dx:
            ok = ok & (bx + dx >= 0) & (bx + dx < fx_size)
        return ok

    def peer(d):
        dy, dx = d
        cross = core if dy == 1 else (1 - core if dy == -1 else 0)
        return (g + cross - 2 * g * cross, bx + dx, by + dy)

    partner = (1 - g, bx, by)

    def ext_copy(d):
        s = (-d[0], -d[1])
        ys, ny = E_SRC_Y[d[0]]
        xs, nx = E_SRC_X[d[1]]
        yd, _ = E_DST_Y[s[0]]
        xd, _ = E_DST_X[s[1]]
        return pltpu.make_async_remote_copy(
            ext.at[pl.ds(ys, ny), pl.ds(xs, nx), :],
            ext.at[pl.ds(yd, ny), pl.ds(xd, nx), :],
            e_send.at[INDEX[d]], e_recv.at[INDEX[s]],
            device_id=peer(d), device_id_type=MESH)

    def landing(s):
        if s[0] == 0:
            return got_x.at[(s[1] + 1) // 2]
        if s[1] == 0:
            return got_y.at[(s[0] + 1) // 2]
        return got_c.at[(s[0] + 1) // 2, (s[1] + 1) // 2]

    def corr_copies(d):
        s = (-d[0], -d[1])
        ys, ny = C_SRC_Y[d[0]]
        xs, nx = C_SRC_X[d[1]]
        return (
            pltpu.make_async_remote_copy(
                scale.at[0 if d[0] else 1], got_scale.at[INDEX[s]],
                s_send.at[INDEX[d]], s_recv.at[INDEX[s]],
                device_id=peer(d), device_id_type=MESH),
            pltpu.make_async_remote_copy(
                quant.at[pl.ds(ys, ny), pl.ds(xs, nx), :], landing(s),
                c_send.at[INDEX[d]], c_recv.at[INDEX[s]],
                device_id=peer(d), device_id_type=MESH),
        )

    def each(order, action):
        for d in order:
            @pl.when(exists(d))
            def _(d=d):
                action(d)

    def corners(leaving, action):
        for d in CORNERS:
            side = core if d[0] == 1 else 1 - core

            @pl.when(exists(d) & (side == leaving))
            def _(d=d):
                action(d)

    def send_ext():
        start = lambda d: ext_copy(d).start()
        each(Y_FACES, start)
        corners(1, start)
        each(X_FACES, start)
        corners(0, start)

    est_copy = pltpu.make_async_copy(est_any, block.at[:, 0:32, :], own_sem.at[0])
    est_copy.start()
    own_images = pltpu.make_async_copy(img_any, img_ref, own_sem.at[1])
    own_images.start()
    kern[...] = jnp.zeros_like(kern)
    ext[...] = jnp.zeros_like(ext)

    barrier = pltpu.get_barrier_semaphore()
    count = jnp.int32(1)
    for d in DIRS:
        count = count + exists(d).astype(jnp.int32)
    pl.semaphore_signal(barrier, inc=1, device_id=partner, device_id_type=MESH)
    each(DIRS, lambda d: pl.semaphore_signal(
        barrier, inc=1, device_id=peer(d), device_id_type=MESH))


    flat = block.reshape(32 * 40, 128)
    est_copy.wait()

    def load_est(y, _):
        row = flat[pl.ds(y, 32, stride=40), :]
        joined[pl.ds(pl.multiple_of(y * 32, 32), 32), :] = row
        ext[pl.ds(y + 16, 1), 16:48, :] = row.astype(BF16)[None]
        return 0

    lax.fori_loop(0, 32, load_est, 0, unroll=4)

    lane = lax.broadcasted_iota(jnp.int32, (16, 128), 1)
    row16 = lax.broadcasted_iota(jnp.int32, (16, 128), 0)
    for k in range(3):
        taps = psf_ref[k]
        kern[pl.ds(own + k, 1), 0:3, 0:31] = (taps / jnp.sum(taps, axis=-1, keepdims=True))[None]
        low = jnp.zeros((16, 128), jnp.int32)
        top = jnp.zeros((16, 128), jnp.int32)
        for jy in range(3):
            for jx in range(3):
                px = bx + (jx - 1)
                py = by + (jy - 1)
                inside = (px >= 0) & (px < fx_size) & (py >= 0) & (py < fy_size)
                cx = jnp.clip(px, 0, fx_size - 1)
                cy = jnp.clip(py, 0, fy_size - 1)
                here = row16 == jy * 3 + jx
                start = lo_ref[k, cx, cy]
                span = len_ref[k, cx, cy] * inside.astype(jnp.int32)
                low = jnp.where(here, start, low)
                top = jnp.where(here, start + span, top)
        masks[pl.ds(own + k, 1)] = jnp.where(
            (lane >= low) & (lane < top), 1.0, 0.0).astype(BF16)[None]

    pl.semaphore_wait(barrier, count)

    send_ext()
    kern_copy = pltpu.make_async_remote_copy(
        kern.at[pl.ds(own, 3)], kern.at[pl.ds(own, 3)],
        v_send.at[3], v_recv.at[3], device_id=partner, device_id_type=MESH)
    mask_copy = pltpu.make_async_remote_copy(
        masks.at[pl.ds(own, 3)], masks.at[pl.ds(own, 3)],
        v_send.at[4], v_recv.at[4], device_id=partner, device_id_type=MESH)

    def img_copy(i):
        return pltpu.make_async_remote_copy(
            img_pack.at[i], img_got.at[i], v_send.at[i], v_recv.at[i],
            device_id=partner, device_id_type=MESH)

    kern_copy.start()
    mask_copy.start()

    low_half = lax.broadcasted_iota(jnp.int32, (64, 128), 1) < 64
    own_images.wait()
    for i in range(3):
        kept = jnp.broadcast_to(masks[own + i, 4:5, :].astype(F32), (64, 128)) > 0.5

        def fold(c, _, i=i, kept=kept):
            r = pl.multiple_of(c * 64, 64)
            first = jnp.where(kept, img_ref[i, pl.ds(r, 64), :].astype(F32), 0.0)
            second = jnp.where(kept, img_ref[i, pl.ds(r + 512, 64), :].astype(F32), 0.0)
            stay = jnp.where(low_half, first, second)
            move = jnp.where(low_half, second, first)
            img_pack[i, pl.ds(r, 64), :] = (stay + pltpu.roll(move, 64, 1)).astype(BF16)
            return 0

        lax.fori_loop(0, 8, fold, 0, unroll=2)
        img_copy(i).start()

    for d in DIRS:
        @pl.when(jnp.logical_not(exists(d)))
        def _(d=d):
            ref = landing(d)
            ref[...] = jnp.zeros(ref.shape, I16)
            got_scale[INDEX[d]] = jnp.zeros((8, 128), F32)

    kern_copy.wait()
    mask_copy.wait()

    zr = lax.broadcasted_iota(jnp.int32, (128, 128), 0)
    zc = lax.broadcasted_iota(jnp.int32, (128, 128), 1)
    near = (zc - zr <= 15) & (zr - zc <= 15)
    mz[...] = jnp.zeros_like(mz)

    def banded(row):
        return pltpu.roll(jnp.broadcast_to(row, (32, 128)), 1, 1, stride=1, stride_axis=0)

    lane32 = lax.broadcasted_iota(jnp.int32, (32, 128), 1)
    pos32 = lax.broadcasted_iota(jnp.int32, (32, 128), 0)

    def side_sums(row):
        taps = jnp.broadcast_to(row, (32, 128))
        before = jnp.sum(jnp.where(lane32 >= pos32 + 16, taps, 0.0), axis=1, keepdims=True)
        after = jnp.sum(jnp.where(lane32 <= pos32 - 17, taps, 0.0), axis=1, keepdims=True)
        middle = jnp.sum(
            jnp.where((lane32 < pos32 + 16) & (lane32 > pos32 - 17), taps, 0.0),
            axis=1, keepdims=True)
        return before, middle, after

    def tables(k, carry):
        sums_x, sums_y = carry
        rows = kern[k]
        near_x = rows[0:1].astype(BF16).astype(F32)
        near_y = rows[1:2].astype(BF16).astype(F32)
        near_z = rows[2:3].astype(BF16).astype(F32)
        gain = (jnp.sum(near_x, axis=1, keepdims=True)
                * jnp.sum(near_y, axis=1, keepdims=True)
                * jnp.sum(near_z, axis=1, keepdims=True))
        tx = banded(near_x)
        ty = banded(near_y)
        r = pl.multiple_of(k * 32, 32)
        fxt[pl.ds(r, 32), :] = tx.astype(BF16)
        fyt[k] = ty.astype(BF16)
        tpose[pl.ds(r, 32), :] = tx
        byt[k] = jnp.concatenate([ty, jnp.zeros((96, 128), F32)], axis=0).T[0:64, :].astype(BF16)
        tz = pltpu.roll(jnp.broadcast_to(near_z, (128, 128)), 113, 1, stride=1, stride_axis=0)
        tz = jnp.where(near, tz, 0.0)
        bzt[k] = tz.astype(BF16)
        fzt[k] = tz.T.astype(BF16)
        m = masks[k]
        mz[pl.ds(pl.multiple_of(k * 16, 16), 16), :] = dot(
            m, bzt[k]) / gain
        part = lane32 - k * 16
        mine = (part >= 0) & (part < 9)
        px = lax.rem(part + 96, 3)
        py = (part + 96) // 3 - 32
        for j, col in enumerate(side_sums(near_x)):
            sums_x = jnp.where(mine & (px == j), col, sums_x)
        for j, col in enumerate(side_sums(near_y)):
            sums_y = jnp.where(mine & (py == j), col, sums_y)
        return sums_x, sums_y

    zero = jnp.zeros((32, 128), F32)
    sums_x, sums_y = lax.fori_loop(0, 6, tables, (zero, zero))
    txs[...] = sums_x
    tys[...] = sums_y
    bxt[:, 0:128] = tpose[0:128, :].T[0:64].astype(BF16)
    bxt[:, 128:256] = tpose[128:256, :].T[0:64].astype(BF16)

    def weigh(q, _):
        parts = []
        for j in range(8):
            parts.append(txs[...] * tys[pl.ds(q * 8 + j, 1), :])
        w = jnp.dot(jnp.concatenate(parts, axis=0), mz[...],
                    preferred_element_type=F32, precision=lax.Precision.HIGHEST)
        low_inv[pl.ds(pl.multiple_of(q * 256, 256), 256), :] = 1.0 / (w + 0.5)
        return 0

    lax.fori_loop(0, 4, weigh, 0)

    def forward_y(k, p):
        cols = jnp.concatenate(
            [wide_a[pl.ds(k * 32 + p * 2 + j, 64, stride=PITCH_A), :].astype(BF16)
             for j in range(2)], axis=1)
        out = dot(fyt[k][:, 0:64], cols).astype(BF16)
        rows_u[p * 64:p * 64 + 32, :] = out[:, 0:128]
        rows_u[p * 64 + 32:p * 64 + 64, :] = out[:, 128:256]

    def backward_y(k, p):
        cols = jnp.concatenate(
            [rows_v[p * 64 + j * 32:p * 64 + j * 32 + 32, :] for j in range(2)], axis=1)
        out = dot(byt[k][:, 0:32], cols)
        for j in range(2):
            r = pl.multiple_of((k * 32 + p * 2 + j) * PITCH_B, 4)
            wide_b[pl.ds(r, 64), :] = out[:, j * 128:j * 128 + 128]

    def middle(k, images):
        covered = masks[k, 4:5, :].astype(F32) > 0.5
        for c in range(4):
            part = slice(c * 256, c * 256 + 256)
            f = dot(rows_u[part, :], fzt[k])
            pic = jnp.where(covered, images[part, :].astype(F32), 0.0)
            rows_r[part, :] = (pic / f).astype(BF16)
        for c in range(4):
            part = slice(c * 256, c * 256 + 256)
            rows_v[part, :] = dot(rows_r[part, :], bzt[k]).astype(BF16)

    def view_step(k, last, images):
        for p in range(16):
            forward_y(k, p)
            backward_y(last, p)
        middle(k, images)

    for step in range(ITERS):
        def pass_x(p, _):
            cols = jnp.concatenate([ext[p * 2], ext[p * 2 + 1]], axis=1)
            out = dot(fxt[:, 0:64], cols)
            for j in range(2):
                r = pl.multiple_of((p * 2 + j) * PITCH_A, 4)
                wide_a[pl.ds(r, 192), :] = out[:, j * 128:j * 128 + 128]
            return 0

        each(X_FACES, lambda d: recv_ext(ext_copy, d))
        lax.fori_loop(8, 24, pass_x, 0, unroll=8)
        each(NOT_X_FACES, lambda d: recv_ext(ext_copy, d))
        lax.fori_loop(0, 8, pass_x, 0, unroll=8)
        lax.fori_loop(24, 32, pass_x, 0, unroll=8)

        for p in range(16):
            forward_y(own, p)
        middle(own, img_ref.at[0])

        def own_views(n, _):
            view_step(own + n, own + n - 1, img_ref.at[n])
            return 0

        lax.fori_loop(1, 3, own_views, 0)

        if step == 0:
            for i in range(3):
                img_copy(i).wait()

                def unfold(c, _, i=i):
                    r = pl.multiple_of(c * 64, 64)
                    stay = img_got[i, pl.ds(r, 64), :].astype(F32)
                    move = pltpu.roll(stay, 64, 1)
                    img2[i, pl.ds(r, 64), :] = jnp.where(low_half, stay, move).astype(BF16)
                    img2[i, pl.ds(r + 512, 64), :] = jnp.where(low_half, move, stay).astype(BF16)
                    return 0

                lax.fori_loop(0, 8, unfold, 0, unroll=2)

        def other_views(n, _):
            view_step(oth + n, jnp.where(n == 0, own + 2, oth + n - 1), img2.at[n])
            return 0

        lax.fori_loop(0, 3, other_views, 0)
        for p in range(16):
            backward_y(oth + 2, p)

        def back_x(p, peak):
            pair = [wide_b[pl.ds(p * 2 + j, 192, stride=PITCH_B), :] for j in range(2)]
            hi, lo = split(jnp.concatenate(pair, axis=1))
            th = bxt[:, 0:192]
            out = dot(th, hi) + dot(th, lo)
            for j in range(2):
                part = out[:, j * 128:j * 128 + 128]
                corr[p * 2 + j] = part
                peak = jnp.maximum(peak, part)
            return peak

        def gain_of(peak, slot):
            peak = jnp.max(jnp.max(peak, axis=0, keepdims=True), axis=1, keepdims=True)
            peak = jnp.maximum(peak, 1e-30)
            scale[slot] = jnp.broadcast_to(peak * (1.0 / QMAX), (8, 128))
            return jnp.broadcast_to(QMAX / peak, (16, 128))

        def put(y, x, gain):
            quant[y, x:x + 16, :] = jnp.round(
                corr[y, x:x + 16, :] * gain).astype(jnp.int32).astype(I16)

        if step > 0:
            each(DIRS, lambda d: [c.wait_send() for c in corr_copies(d)])
        zeros = jnp.zeros((64, 128), F32)
        peak = lax.fori_loop(0, 8, back_x, zeros, unroll=4)
        peak = lax.fori_loop(24, 32, back_x, peak, unroll=4)
        outer = gain_of(peak, 0)

        def code_outer(y, _):
            for x in (0, 16, 32, 48):
                put(y, x, outer)
                put(y + 48, x, outer)
            return 0

        lax.fori_loop(0, 16, code_outer, 0, unroll=2)
        start = lambda d: [c.start() for c in corr_copies(d)]
        each(Y_FACES, start)
        corners(1, start)
        corners(0, start)

        peak = lax.fori_loop(8, 24, back_x, zeros, unroll=4)
        inner = gain_of(peak, 1)

        def code_inner(y, _):
            put(y, 0, inner)
            put(y, 48, inner)
            return 0

        lax.fori_loop(16, 48, code_inner, 0, unroll=4)
        each(X_FACES, lambda d: [c.start() for c in corr_copies(d)])
        each(DIRS, lambda d: ext_copy(d).wait_send())
        each(DIRS, lambda d: recv_corr(corr_copies, d))

        factors = {d: jnp.broadcast_to(got_scale[INDEX[d], 0:1, :], (16, 128)) for d in DIRS}

        def wide(ref):
            return ref.astype(jnp.int32).astype(F32)

        def finish(y, i, sy):
            left = corr[y + 16, 16:32, :] + wide(got_x[0, y]) * factors[(0, -1)]
            right = corr[y + 16, 32:48, :] + wide(got_x[1, y]) * factors[(0, 1)]
            if sy:
                s = (sy + 1) // 2
                left = left + wide(got_y[s, i, 0:16]) * factors[(sy, 0)]
                left = left + wide(got_c[s, 0, i]) * factors[(sy, -1)]
                right = right + wide(got_y[s, i, 16:32]) * factors[(sy, 0)]
                right = right + wide(got_c[s, 1, i]) * factors[(sy, 1)]
            total = jnp.concatenate([left, right], axis=0)
            r = pl.multiple_of(y * 32, 32)
            new = joined[pl.ds(r, 32), :] * (total + 0.5) * low_inv[pl.ds(r, 32), :]
            if step + 1 < ITERS:
                joined[pl.ds(r, 32), :] = new
                ext[pl.ds(y + 16, 1), 16:48, :] = new.astype(BF16)[None]
            else:
                flat[pl.ds(y, 32, stride=40), :] = new

        def edges(i, _):
            finish(i, i, -1)
            finish(i + 17, i, 1)
            return 0

        lax.fori_loop(0, 15, edges, 0)
        finish(15, 0, 0)
        finish(16, 0, 0)
        if step + 1 < ITERS:
            send_ext()

    def put_out(x, _):
        out_ref[pl.ds(x * 4, 4)] = block[pl.ds(x * 4, 4), 0:32, :]
        return 0

    lax.fori_loop(0, 8, put_out, 0, unroll=2)
    each(DIRS, lambda d: [c.wait_send() for c in corr_copies(d)])


def recv_ext(copy, s):
    copy((-s[0], -s[1])).wait_recv()


def recv_corr(copies, s):
    for c in copies((-s[0], -s[1])):
        c.wait_recv()


def body(fx_size, fy_size, estimate, images, psf, cover_lo, cover_len):
    vmem = pl.BlockSpec(memory_space=pltpu.VMEM)
    smem = pl.BlockSpec(memory_space=pltpu.SMEM)
    anywhere = pl.BlockSpec(memory_space=pltpu.HBM)
    dma = pltpu.SemaphoreType.DMA
    out = pl.pallas_call(
        functools.partial(kernel, fx_size, fy_size),
        out_shape=jax.ShapeDtypeStruct((32, 32, 128), F32),
        in_specs=[anywhere, anywhere, vmem, smem, smem],
        out_specs=vmem,
        scratch_shapes=[
            pltpu.VMEM((32, 40, 128), F32),
            pltpu.VMEM((3, 1024, 128), BF16),
            pltpu.VMEM((3, 512, 128), BF16),
            pltpu.VMEM((3, 512, 128), BF16),
            pltpu.VMEM((64, 64, 128), BF16),
            pltpu.VMEM((1024, 128), F32),
            pltpu.VMEM((3, 1024, 128), BF16),
            pltpu.VMEM((6, 8, 128), F32),
            pltpu.VMEM((6, 16, 128), BF16),
            pltpu.VMEM((64 * PITCH_A, 128), F32),
            pltpu.VMEM((192 * PITCH_B, 128), F32),
            pltpu.VMEM((64, 64, 128), F32),
            pltpu.VMEM((64, 64, 128), I16),
            pltpu.VMEM((2, 32, 16, 128), I16),
            pltpu.VMEM((2, 15, 32, 128), I16),
            pltpu.VMEM((2, 2, 15, 16, 128), I16),
            pltpu.VMEM((2, 8, 128), F32),
            pltpu.VMEM((8, 8, 128), F32),
            pltpu.VMEM((192, 128), BF16),
            pltpu.VMEM((6, 32, 128), BF16),
            pltpu.VMEM((6, 128, 128), BF16),
            pltpu.VMEM((6, 128, 128), BF16),
            pltpu.VMEM((6, 64, 128), BF16),
            pltpu.VMEM((64, 256), BF16),
            pltpu.VMEM((1024, 128), F32),
            pltpu.VMEM((128, 128), F32),
            pltpu.VMEM((32, 128), F32),
            pltpu.VMEM((32, 128), F32),
            pltpu.VMEM((256, 128), F32),
            pltpu.VMEM((1024, 128), BF16),
            pltpu.VMEM((1024, 128), BF16),
            pltpu.VMEM((1024, 128), BF16),
            dma((8,)), dma((8,)), dma((8,)), dma((8,)),
            dma((8,)), dma((8,)), dma((5,)), dma((5,)), dma((2,)),
        ],
        compiler_params=pltpu.CompilerParams(
            collective_id=0, has_side_effects=True, vmem_limit_bytes=40 << 20),
    )(
        estimate, images.reshape(3, 1024, 128), psf, cover_lo, cover_len)
    return out


def solution(mesh):
    return jax.shard_map(
        functools.partial(body, mesh.shape["fx"], mesh.shape["fy"]),
        mesh=mesh,
        in_specs=(
            P("fx", "fy", None),
            P("view", "fx", "fy", None),
            P("view", None, None),
            P("view", None, None),
            P("view", None, None),
        ),
        out_specs=P("fx", "fy", None),
        check_vma=False,
    )
```

```python
import functools

import jax
import jax.numpy as jnp
from jax import lax
from jax.experimental import pallas as pl
from jax.experimental.pallas import tpu as pltpu
from jax.sharding import PartitionSpec as P

ITERS = 2
MESH = pl.DeviceIdType.MESH
BF16 = jnp.bfloat16
F32 = jnp.float32
I16 = jnp.int16
QMAX = 32000.0
PITCH_A = 196
PITCH_B = 68

DIRS = tuple((dy, dx) for dy in (-1, 0, 1) for dx in (-1, 0, 1) if dy or dx)
INDEX = {d: i for i, d in enumerate(DIRS)}
X_FACES = ((0, 1), (0, -1))
NOT_X_FACES = ((1, 0), (-1, 0), (1, 1), (1, -1), (-1, 1), (-1, -1))
Y_FACES = NOT_X_FACES[:2]
CORNERS = NOT_X_FACES[2:]

E_SRC_Y = {1: (33, 15), -1: (16, 15), 0: (16, 32)}
E_DST_Y = {-1: (1, 15), 1: (48, 15), 0: (16, 32)}
E_SRC_X = {1: (32, 16), -1: (16, 16), 0: (16, 32)}
E_DST_X = {-1: (0, 16), 1: (48, 16), 0: (16, 32)}
C_SRC_Y = {1: (48, 15), -1: (1, 15), 0: (16, 32)}
C_SRC_X = {1: (48, 16), -1: (0, 16), 0: (16, 32)}


def dot(a, b):
    return jnp.dot(a, b, preferred_element_type=F32)


def split(v):
    hi = v.astype(BF16)
    return hi, (v - hi.astype(F32)).astype(BF16)


def kernel(
    fx_size, fy_size,
    est_any, img_any, psf_ref, lo_ref, len_ref, out_ref,
    block, img_ref, img_pack, img_got,
    ext, joined, img2, kern, masks, wide_a, wide_b, corr, quant,
    got_x, got_y, got_c, scale, got_scale,
    fxt, fyt, fzt, bzt, byt, bxt, low_inv, mz, txs, tys, tpose, rows_u, rows_r, rows_v,
    e_send, e_recv, c_send, c_recv, s_send, s_recv, v_send, v_recv, own_sem,
):
    g = lax.axis_index("view")
    bx = lax.axis_index("fx")
    by = lax.axis_index("fy")
    core = lax.rem(by, 2)
    own = g * 3
    oth = 3 - own

    def exists(d):
        dy, dx = d
        ok = jnp.bool_(True)
        if dy:
            ok = ok & (by + dy >= 0) & (by + dy < fy_size)
        if dx:
            ok = ok & (bx + dx >= 0) & (bx + dx < fx_size)
        return ok

    def peer(d):
        dy, dx = d
        cross = core if dy == 1 else (1 - core if dy == -1 else 0)
        return (g + cross - 2 * g * cross, bx + dx, by + dy)

    partner = (1 - g, bx, by)

    def ext_copy(d):
        s = (-d[0], -d[1])
        ys, ny = E_SRC_Y[d[0]]
        xs, nx = E_SRC_X[d[1]]
        yd, _ = E_DST_Y[s[0]]
        xd, _ = E_DST_X[s[1]]
        return pltpu.make_async_remote_copy(
            ext.at[pl.ds(ys, ny), pl.ds(xs, nx), :],
            ext.at[pl.ds(yd, ny), pl.ds(xd, nx), :],
            e_send.at[INDEX[d]], e_recv.at[INDEX[s]],
            device_id=peer(d), device_id_type=MESH)

    def landing(s):
        if s[0] == 0:
            return got_x.at[(s[1] + 1) // 2]
        if s[1] == 0:
            return got_y.at[(s[0] + 1) // 2]
        return got_c.at[(s[0] + 1) // 2, (s[1] + 1) // 2]

    def corr_copies(d):
        s = (-d[0], -d[1])
        ys, ny = C_SRC_Y[d[0]]
        xs, nx = C_SRC_X[d[1]]
        return (
            pltpu.make_async_remote_copy(
                scale.at[0 if d[0] else 1], got_scale.at[INDEX[s]],
                s_send.at[INDEX[d]], s_recv.at[INDEX[s]],
                device_id=peer(d), device_id_type=MESH),
            pltpu.make_async_remote_copy(
                quant.at[pl.ds(ys, ny), pl.ds(xs, nx), :], landing(s),
                c_send.at[INDEX[d]], c_recv.at[INDEX[s]],
                device_id=peer(d), device_id_type=MESH),
        )

    def each(order, action):
        for d in order:
            @pl.when(exists(d))
            def _(d=d):
                action(d)

    def corners(leaving, action):
        for d in CORNERS:
            side = core if d[0] == 1 else 1 - core

            @pl.when(exists(d) & (side == leaving))
            def _(d=d):
                action(d)

    def send_ext():
        start = lambda d: ext_copy(d).start()
        each(Y_FACES, start)
        corners(1, start)
        each(X_FACES, start)
        corners(0, start)

    est_copy = pltpu.make_async_copy(est_any, block.at[:, 0:32, :], own_sem.at[0])
    est_copy.start()
    own_images = pltpu.make_async_copy(img_any, img_ref, own_sem.at[1])
    own_images.start()
    kern[...] = jnp.zeros_like(kern)
    ext[...] = jnp.zeros_like(ext)

    barrier = pltpu.get_barrier_semaphore()
    count = jnp.int32(1)
    for d in DIRS:
        count = count + exists(d).astype(jnp.int32)
    pl.semaphore_signal(barrier, inc=1, device_id=partner, device_id_type=MESH)
    each(DIRS, lambda d: pl.semaphore_signal(
        barrier, inc=1, device_id=peer(d), device_id_type=MESH))


    flat = block.reshape(32 * 40, 128)
    est_copy.wait()

    def load_est(y, _):
        row = flat[pl.ds(y, 32, stride=40), :]
        joined[pl.ds(pl.multiple_of(y * 32, 32), 32), :] = row
        ext[pl.ds(y + 16, 1), 16:48, :] = row.astype(BF16)[None]
        return 0

    lax.fori_loop(0, 32, load_est, 0, unroll=4)

    pl.semaphore_wait(barrier, count)
    send_ext()

    lane = lax.broadcasted_iota(jnp.int32, (16, 128), 1)
    row16 = lax.broadcasted_iota(jnp.int32, (16, 128), 0)
    for k in range(3):
        taps = psf_ref[k]
        kern[pl.ds(own + k, 1), 0:3, 0:31] = (taps / jnp.sum(taps, axis=-1, keepdims=True))[None]
        low = jnp.zeros((16, 128), jnp.int32)
        top = jnp.zeros((16, 128), jnp.int32)
        for jy in range(3):
            for jx in range(3):
                px = bx + (jx - 1)
                py = by + (jy - 1)
                inside = (px >= 0) & (px < fx_size) & (py >= 0) & (py < fy_size)
                cx = jnp.clip(px, 0, fx_size - 1)
                cy = jnp.clip(py, 0, fy_size - 1)
                here = row16 == jy * 3 + jx
                start = lo_ref[k, cx, cy]
                span = len_ref[k, cx, cy] * inside.astype(jnp.int32)
                low = jnp.where(here, start, low)
                top = jnp.where(here, start + span, top)
        masks[pl.ds(own + k, 1)] = jnp.where(
            (lane >= low) & (lane < top), 1.0, 0.0).astype(BF16)[None]

    kern_copy = pltpu.make_async_remote_copy(
        kern.at[pl.ds(own, 3)], kern.at[pl.ds(own, 3)],
        v_send.at[3], v_recv.at[3], device_id=partner, device_id_type=MESH)
    mask_copy = pltpu.make_async_remote_copy(
        masks.at[pl.ds(own, 3)], masks.at[pl.ds(own, 3)],
        v_send.at[4], v_recv.at[4], device_id=partner, device_id_type=MESH)

    def img_copy(i):
        return pltpu.make_async_remote_copy(
            img_pack.at[i], img_got.at[i], v_send.at[i], v_recv.at[i],
            device_id=partner, device_id_type=MESH)

    kern_copy.start()
    mask_copy.start()

    low_half = lax.broadcasted_iota(jnp.int32, (64, 128), 1) < 64
    own_images.wait()
    for i in range(3):
        kept = jnp.broadcast_to(masks[own + i, 4:5, :].astype(F32), (64, 128)) > 0.5

        def fold(c, _, i=i, kept=kept):
            r = pl.multiple_of(c * 64, 64)
            first = jnp.where(kept, img_ref[i, pl.ds(r, 64), :].astype(F32), 0.0)
            second = jnp.where(kept, img_ref[i, pl.ds(r + 512, 64), :].astype(F32), 0.0)
            stay = jnp.where(low_half, first, second)
            move = jnp.where(low_half, second, first)
            img_pack[i, pl.ds(r, 64), :] = (stay + pltpu.roll(move, 64, 1)).astype(BF16)
            return 0

        lax.fori_loop(0, 8, fold, 0, unroll=2)
        img_copy(i).start()

    for d in DIRS:
        @pl.when(jnp.logical_not(exists(d)))
        def _(d=d):
            ref = landing(d)
            ref[...] = jnp.zeros(ref.shape, I16)
            got_scale[INDEX[d]] = jnp.zeros((8, 128), F32)

    kern_copy.wait()
    mask_copy.wait()

    zr = lax.broadcasted_iota(jnp.int32, (128, 128), 0)
    zc = lax.broadcasted_iota(jnp.int32, (128, 128), 1)
    near = (zc - zr <= 15) & (zr - zc <= 15)
    mz[...] = jnp.zeros_like(mz)

    def banded(row):
        return pltpu.roll(jnp.broadcast_to(row, (32, 128)), 1, 1, stride=1, stride_axis=0)

    lane32 = lax.broadcasted_iota(jnp.int32, (32, 128), 1)
    pos32 = lax.broadcasted_iota(jnp.int32, (32, 128), 0)

    def side_sums(row):
        taps = jnp.broadcast_to(row, (32, 128))
        before = jnp.sum(jnp.where(lane32 >= pos32 + 16, taps, 0.0), axis=1, keepdims=True)
        after = jnp.sum(jnp.where(lane32 <= pos32 - 17, taps, 0.0), axis=1, keepdims=True)
        middle = jnp.sum(
            jnp.where((lane32 < pos32 + 16) & (lane32 > pos32 - 17), taps, 0.0),
            axis=1, keepdims=True)
        return before, middle, after

    def tables(k, carry):
        sums_x, sums_y = carry
        rows = kern[k]
        near_x = rows[0:1].astype(BF16).astype(F32)
        near_y = rows[1:2].astype(BF16).astype(F32)
        near_z = rows[2:3].astype(BF16).astype(F32)
        gain = (jnp.sum(near_x, axis=1, keepdims=True)
                * jnp.sum(near_y, axis=1, keepdims=True)
                * jnp.sum(near_z, axis=1, keepdims=True))
        tx = banded(near_x)
        ty = banded(near_y)
        r = pl.multiple_of(k * 32, 32)
        fxt[pl.ds(r, 32), :] = tx.astype(BF16)
        fyt[k] = ty.astype(BF16)
        tpose[pl.ds(r, 32), :] = tx
        byt[k] = jnp.concatenate([ty, jnp.zeros((96, 128), F32)], axis=0).T[0:64, :].astype(BF16)
        tz = pltpu.roll(jnp.broadcast_to(near_z, (128, 128)), 113, 1, stride=1, stride_axis=0)
        tz = jnp.where(near, tz, 0.0)
        bzt[k] = tz.astype(BF16)
        fzt[k] = tz.T.astype(BF16)
        m = masks[k]
        mz[pl.ds(pl.multiple_of(k * 16, 16), 16), :] = dot(
            m, bzt[k]) / gain
        part = lane32 - k * 16
        mine = (part >= 0) & (part < 9)
        px = lax.rem(part + 96, 3)
        py = (part + 96) // 3 - 32
        for j, col in enumerate(side_sums(near_x)):
            sums_x = jnp.where(mine & (px == j), col, sums_x)
        for j, col in enumerate(side_sums(near_y)):
            sums_y = jnp.where(mine & (py == j), col, sums_y)
        return sums_x, sums_y

    zero = jnp.zeros((32, 128), F32)
    sums_x, sums_y = lax.fori_loop(0, 6, tables, (zero, zero))
    txs[...] = sums_x
    tys[...] = sums_y
    bxt[:, 0:128] = tpose[0:128, :].T[0:64].astype(BF16)
    bxt[:, 128:256] = tpose[128:256, :].T[0:64].astype(BF16)

    def weigh(q, _):
        parts = []
        for j in range(8):
            parts.append(txs[...] * tys[pl.ds(q * 8 + j, 1), :])
        w = jnp.dot(jnp.concatenate(parts, axis=0), mz[...],
                    preferred_element_type=F32, precision=lax.Precision.HIGHEST)
        low_inv[pl.ds(pl.multiple_of(q * 256, 256), 256), :] = 1.0 / (w + 0.5)
        return 0

    lax.fori_loop(0, 4, weigh, 0)

    def forward_y(k, p):
        cols = jnp.concatenate(
            [wide_a[pl.ds(k * 32 + p * 2 + j, 64, stride=PITCH_A), :].astype(BF16)
             for j in range(2)], axis=1)
        out = dot(fyt[k][:, 0:64], cols).astype(BF16)
        rows_u[p * 64:p * 64 + 32, :] = out[:, 0:128]
        rows_u[p * 64 + 32:p * 64 + 64, :] = out[:, 128:256]

    def backward_y(k, p):
        cols = jnp.concatenate(
            [rows_v[p * 64 + j * 32:p * 64 + j * 32 + 32, :] for j in range(2)], axis=1)
        out = dot(byt[k][:, 0:32], cols)
        for j in range(2):
            r = pl.multiple_of((k * 32 + p * 2 + j) * PITCH_B, 4)
            wide_b[pl.ds(r, 64), :] = out[:, j * 128:j * 128 + 128]

    def middle(k, images):
        covered = masks[k, 4:5, :].astype(F32) > 0.5
        for c in range(4):
            part = slice(c * 256, c * 256 + 256)
            f = dot(rows_u[part, :], fzt[k])
            pic = jnp.where(covered, images[part, :].astype(F32), 0.0)
            rows_r[part, :] = (pic / f).astype(BF16)
        for c in range(4):
            part = slice(c * 256, c * 256 + 256)
            rows_v[part, :] = dot(rows_r[part, :], bzt[k]).astype(BF16)

    def view_step(k, last, images):
        for p in range(16):
            forward_y(k, p)
            backward_y(last, p)
        middle(k, images)

    for step in range(ITERS):
        def pass_x(p, _):
            cols = jnp.concatenate([ext[p * 2], ext[p * 2 + 1]], axis=1)
            out = dot(fxt[:, 0:64], cols)
            for j in range(2):
                r = pl.multiple_of((p * 2 + j) * PITCH_A, 4)
                wide_a[pl.ds(r, 192), :] = out[:, j * 128:j * 128 + 128]
            return 0

        each(X_FACES, lambda d: recv_ext(ext_copy, d))
        lax.fori_loop(8, 24, pass_x, 0, unroll=8)
        each(NOT_X_FACES, lambda d: recv_ext(ext_copy, d))
        lax.fori_loop(0, 8, pass_x, 0, unroll=8)
        lax.fori_loop(24, 32, pass_x, 0, unroll=8)

        for p in range(16):
            forward_y(own, p)
        middle(own, img_ref.at[0])

        def own_views(n, _):
            view_step(own + n, own + n - 1, img_ref.at[n])
            return 0

        lax.fori_loop(1, 3, own_views, 0)

        if step == 0:
            for i in range(3):
                img_copy(i).wait()

                def unfold(c, _, i=i):
                    r = pl.multiple_of(c * 64, 64)
                    stay = img_got[i, pl.ds(r, 64), :].astype(F32)
                    move = pltpu.roll(stay, 64, 1)
                    img2[i, pl.ds(r, 64), :] = jnp.where(low_half, stay, move).astype(BF16)
                    img2[i, pl.ds(r + 512, 64), :] = jnp.where(low_half, move, stay).astype(BF16)
                    return 0

                lax.fori_loop(0, 8, unfold, 0, unroll=2)

        def other_views(n, _):
            view_step(oth + n, jnp.where(n == 0, own + 2, oth + n - 1), img2.at[n])
            return 0

        lax.fori_loop(0, 3, other_views, 0)
        for p in range(16):
            backward_y(oth + 2, p)

        def back_x(p, peak):
            pair = [wide_b[pl.ds(p * 2 + j, 192, stride=PITCH_B), :] for j in range(2)]
            hi, lo = split(jnp.concatenate(pair, axis=1))
            th = bxt[:, 0:192]
            out = dot(th, hi) + dot(th, lo)
            for j in range(2):
                part = out[:, j * 128:j * 128 + 128]
                corr[p * 2 + j] = part
                peak = jnp.maximum(peak, part)
            return peak

        def gain_of(peak, slot):
            peak = jnp.max(jnp.max(peak, axis=0, keepdims=True), axis=1, keepdims=True)
            peak = jnp.maximum(peak, 1e-30)
            scale[slot] = jnp.broadcast_to(peak * (1.0 / QMAX), (8, 128))
            return jnp.broadcast_to(QMAX / peak, (16, 128))

        def put(y, x, gain):
            quant[y, x:x + 16, :] = jnp.round(
                corr[y, x:x + 16, :] * gain).astype(jnp.int32).astype(I16)

        if step > 0:
            each(DIRS, lambda d: [c.wait_send() for c in corr_copies(d)])
        zeros = jnp.zeros((64, 128), F32)
        peak = lax.fori_loop(0, 8, back_x, zeros, unroll=4)
        peak = lax.fori_loop(24, 32, back_x, peak, unroll=4)
        outer = gain_of(peak, 0)

        def code_outer(y, _):
            for x in (0, 16, 32, 48):
                put(y, x, outer)
                put(y + 48, x, outer)
            return 0

        lax.fori_loop(0, 16, code_outer, 0, unroll=2)
        start = lambda d: [c.start() for c in corr_copies(d)]
        each(Y_FACES, start)
        corners(1, start)
        corners(0, start)

        peak = lax.fori_loop(8, 24, back_x, zeros, unroll=4)
        inner = gain_of(peak, 1)

        def code_inner(y, _):
            put(y, 0, inner)
            put(y, 48, inner)
            return 0

        lax.fori_loop(16, 48, code_inner, 0, unroll=4)
        each(X_FACES, lambda d: [c.start() for c in corr_copies(d)])
        each(DIRS, lambda d: ext_copy(d).wait_send())
        each(DIRS, lambda d: recv_corr(corr_copies, d))

        factors = {d: jnp.broadcast_to(got_scale[INDEX[d], 0:1, :], (16, 128)) for d in DIRS}

        def wide(ref):
            return ref.astype(jnp.int32).astype(F32)

        def finish(y, i, sy):
            left = corr[y + 16, 16:32, :] + wide(got_x[0, y]) * factors[(0, -1)]
            right = corr[y + 16, 32:48, :] + wide(got_x[1, y]) * factors[(0, 1)]
            if sy:
                s = (sy + 1) // 2
                left = left + wide(got_y[s, i, 0:16]) * factors[(sy, 0)]
                left = left + wide(got_c[s, 0, i]) * factors[(sy, -1)]
                right = right + wide(got_y[s, i, 16:32]) * factors[(sy, 0)]
                right = right + wide(got_c[s, 1, i]) * factors[(sy, 1)]
            total = jnp.concatenate([left, right], axis=0)
            r = pl.multiple_of(y * 32, 32)
            new = joined[pl.ds(r, 32), :] * (total + 0.5) * low_inv[pl.ds(r, 32), :]
            if step + 1 < ITERS:
                joined[pl.ds(r, 32), :] = new
                ext[pl.ds(y + 16, 1), 16:48, :] = new.astype(BF16)[None]
            else:
                flat[pl.ds(y, 32, stride=40), :] = new

        def edges(i, _):
            finish(i, i, -1)
            finish(i + 17, i, 1)
            return 0

        lax.fori_loop(0, 15, edges, 0)
        finish(15, 0, 0)
        finish(16, 0, 0)
        if step + 1 < ITERS:
            send_ext()

    def put_out(x, _):
        out_ref[pl.ds(x * 4, 4)] = block[pl.ds(x * 4, 4), 0:32, :]
        return 0

    lax.fori_loop(0, 8, put_out, 0, unroll=2)
    each(DIRS, lambda d: [c.wait_send() for c in corr_copies(d)])


def recv_ext(copy, s):
    copy((-s[0], -s[1])).wait_recv()


def recv_corr(copies, s):
    for c in copies((-s[0], -s[1])):
        c.wait_recv()


def body(fx_size, fy_size, estimate, images, psf, cover_lo, cover_len):
    vmem = pl.BlockSpec(memory_space=pltpu.VMEM)
    smem = pl.BlockSpec(memory_space=pltpu.SMEM)
    anywhere = pl.BlockSpec(memory_space=pltpu.HBM)
    dma = pltpu.SemaphoreType.DMA
    out = pl.pallas_call(
        functools.partial(kernel, fx_size, fy_size),
        out_shape=jax.ShapeDtypeStruct((32, 32, 128), F32),
        in_specs=[anywhere, anywhere, vmem, smem, smem],
        out_specs=vmem,
        scratch_shapes=[
            pltpu.VMEM((32, 40, 128), F32),
            pltpu.VMEM((3, 1024, 128), BF16),
            pltpu.VMEM((3, 512, 128), BF16),
            pltpu.VMEM((3, 512, 128), BF16),
            pltpu.VMEM((64, 64, 128), BF16),
            pltpu.VMEM((1024, 128), F32),
            pltpu.VMEM((3, 1024, 128), BF16),
            pltpu.VMEM((6, 8, 128), F32),
            pltpu.VMEM((6, 16, 128), BF16),
            pltpu.VMEM((64 * PITCH_A, 128), F32),
            pltpu.VMEM((192 * PITCH_B, 128), F32),
            pltpu.VMEM((64, 64, 128), F32),
            pltpu.VMEM((64, 64, 128), I16),
            pltpu.VMEM((2, 32, 16, 128), I16),
            pltpu.VMEM((2, 15, 32, 128), I16),
            pltpu.VMEM((2, 2, 15, 16, 128), I16),
            pltpu.VMEM((2, 8, 128), F32),
            pltpu.VMEM((8, 8, 128), F32),
            pltpu.VMEM((192, 128), BF16),
            pltpu.VMEM((6, 32, 128), BF16),
            pltpu.VMEM((6, 128, 128), BF16),
            pltpu.VMEM((6, 128, 128), BF16),
            pltpu.VMEM((6, 64, 128), BF16),
            pltpu.VMEM((64, 256), BF16),
            pltpu.VMEM((1024, 128), F32),
            pltpu.VMEM((128, 128), F32),
            pltpu.VMEM((32, 128), F32),
            pltpu.VMEM((32, 128), F32),
            pltpu.VMEM((256, 128), F32),
            pltpu.VMEM((1024, 128), BF16),
            pltpu.VMEM((1024, 128), BF16),
            pltpu.VMEM((1024, 128), BF16),
            dma((8,)), dma((8,)), dma((8,)), dma((8,)),
            dma((8,)), dma((8,)), dma((5,)), dma((5,)), dma((2,)),
        ],
        compiler_params=pltpu.CompilerParams(
            collective_id=0, has_side_effects=True, vmem_limit_bytes=40 << 20),
    )(
        *(pltpu.with_memory_space_constraint(a, pltpu.HBM) for a in (
            estimate, images.reshape(3, 1024, 128), psf, cover_lo, cover_len)))
    return out


def solution(mesh):
    return jax.shard_map(
        functools.partial(body, mesh.shape["fx"], mesh.shape["fy"]),
        mesh=mesh,
        in_specs=(
            P("fx", "fy", None),
            P("view", "fx", "fy", None),
            P("view", None, None),
            P("view", None, None),
            P("view", None, None),
        ),
        out_specs=P("fx", "fy", None),
        check_vma=False,
    )
```

```python
import functools

import jax
import jax.numpy as jnp
from jax import lax
from jax.experimental import pallas as pl
from jax.experimental.pallas import tpu as pltpu
from jax.sharding import PartitionSpec as P

ITERS = 2
MESH = pl.DeviceIdType.MESH
BF16 = jnp.bfloat16
F32 = jnp.float32
I16 = jnp.int16
QMAX = 32000.0
PITCH_A = 196
PITCH_B = 68

DIRS = tuple((dy, dx) for dy in (-1, 0, 1) for dx in (-1, 0, 1) if dy or dx)
INDEX = {d: i for i, d in enumerate(DIRS)}
X_FACES = ((0, 1), (0, -1))
NOT_X_FACES = ((1, 0), (-1, 0), (1, 1), (1, -1), (-1, 1), (-1, -1))
Y_FACES = NOT_X_FACES[:2]
CORNERS = NOT_X_FACES[2:]

E_SRC_Y = {1: (33, 15), -1: (16, 15), 0: (16, 32)}
E_DST_Y = {-1: (1, 15), 1: (48, 15), 0: (16, 32)}
E_SRC_X = {1: (32, 16), -1: (16, 16), 0: (16, 32)}
E_DST_X = {-1: (0, 16), 1: (48, 16), 0: (16, 32)}
C_SRC_Y = {1: (48, 15), -1: (1, 15), 0: (16, 32)}
C_SRC_X = {1: (48, 16), -1: (0, 16), 0: (16, 32)}


def dot(a, b):
    return jnp.dot(a, b, preferred_element_type=F32)


def split(v):
    hi = v.astype(BF16)
    return hi, (v - hi.astype(F32)).astype(BF16)


def kernel(
    fx_size, fy_size,
    est_any, img_any, psf_ref, lo_ref, len_ref, out_ref,
    block, img_ref, img_pack, img_got,
    ext, joined, img2, kern, masks, wide_a, wide_b, corr, quant,
    got_x, got_y, got_c, scale, got_scale,
    fxt, fyt, fzt, bzt, byt, bxt, low_inv, mz, txs, tys, tpose, rows_u, rows_r, rows_v,
    e_send, e_recv, c_send, c_recv, s_send, s_recv, v_send, v_recv, own_sem,
):
    g = lax.axis_index("view")
    bx = lax.axis_index("fx")
    by = lax.axis_index("fy")
    core = lax.rem(by, 2)
    own = g * 3
    oth = 3 - own

    def exists(d):
        dy, dx = d
        ok = jnp.bool_(True)
        if dy:
            ok = ok & (by + dy >= 0) & (by + dy < fy_size)
        if dx:
            ok = ok & (bx + dx >= 0) & (bx + dx < fx_size)
        return ok

    def peer(d):
        dy, dx = d
        cross = core if dy == 1 else (1 - core if dy == -1 else 0)
        return (g + cross - 2 * g * cross, bx + dx, by + dy)

    partner = (1 - g, bx, by)

    def ext_copy(d):
        s = (-d[0], -d[1])
        ys, ny = E_SRC_Y[d[0]]
        xs, nx = E_SRC_X[d[1]]
        yd, _ = E_DST_Y[s[0]]
        xd, _ = E_DST_X[s[1]]
        return pltpu.make_async_remote_copy(
            ext.at[pl.ds(ys, ny), pl.ds(xs, nx), :],
            ext.at[pl.ds(yd, ny), pl.ds(xd, nx), :],
            e_send.at[INDEX[d]], e_recv.at[INDEX[s]],
            device_id=peer(d), device_id_type=MESH)

    def landing(s):
        if s[0] == 0:
            return got_x.at[(s[1] + 1) // 2]
        if s[1] == 0:
            return got_y.at[(s[0] + 1) // 2]
        return got_c.at[(s[0] + 1) // 2, (s[1] + 1) // 2]

    def corr_copies(d):
        s = (-d[0], -d[1])
        ys, ny = C_SRC_Y[d[0]]
        xs, nx = C_SRC_X[d[1]]
        return (
            pltpu.make_async_remote_copy(
                scale.at[1 - leaving(d) if d[0] else 2], got_scale.at[INDEX[s]],
                s_send.at[INDEX[d]], s_recv.at[INDEX[s]],
                device_id=peer(d), device_id_type=MESH),
            pltpu.make_async_remote_copy(
                quant.at[pl.ds(ys, ny), pl.ds(xs, nx), :], landing(s),
                c_send.at[INDEX[d]], c_recv.at[INDEX[s]],
                device_id=peer(d), device_id_type=MESH),
        )

    def each(order, action):
        for d in order:
            @pl.when(exists(d))
            def _(d=d):
                action(d)

    def leaving(d):
        return core if d[0] == 1 else 1 - core

    def toward(order, out, action):
        for d in order:
            @pl.when(exists(d) & (leaving(d) == out))
            def _(d=d):
                action(d)

    def send_ext():
        start = lambda d: ext_copy(d).start()
        each(Y_FACES, start)
        toward(CORNERS, 1, start)
        each(X_FACES, start)
        toward(CORNERS, 0, start)

    est_copy = pltpu.make_async_copy(est_any, block.at[:, 0:32, :], own_sem.at[0])
    est_copy.start()
    own_images = pltpu.make_async_copy(img_any, img_ref, own_sem.at[1])
    own_images.start()
    kern[...] = jnp.zeros_like(kern)
    ext[...] = jnp.zeros_like(ext)

    barrier = pltpu.get_barrier_semaphore()
    count = jnp.int32(1)
    for d in DIRS:
        count = count + exists(d).astype(jnp.int32)
    pl.semaphore_signal(barrier, inc=1, device_id=partner, device_id_type=MESH)
    each(DIRS, lambda d: pl.semaphore_signal(
        barrier, inc=1, device_id=peer(d), device_id_type=MESH))


    flat = block.reshape(32 * 40, 128)
    est_copy.wait()

    def load_est(y, _):
        row = flat[pl.ds(y, 32, stride=40), :]
        joined[pl.ds(pl.multiple_of(y * 32, 32), 32), :] = row
        ext[pl.ds(y + 16, 1), 16:48, :] = row.astype(BF16)[None]
        return 0

    lax.fori_loop(0, 32, load_est, 0, unroll=4)

    pl.semaphore_wait(barrier, count)
    send_ext()

    lane = lax.broadcasted_iota(jnp.int32, (16, 128), 1)
    row16 = lax.broadcasted_iota(jnp.int32, (16, 128), 0)
    for k in range(3):
        taps = psf_ref[k]
        kern[pl.ds(own + k, 1), 0:3, 0:31] = (taps / jnp.sum(taps, axis=-1, keepdims=True))[None]
        low = jnp.zeros((16, 128), jnp.int32)
        top = jnp.zeros((16, 128), jnp.int32)
        for jy in range(3):
            for jx in range(3):
                px = bx + (jx - 1)
                py = by + (jy - 1)
                inside = (px >= 0) & (px < fx_size) & (py >= 0) & (py < fy_size)
                cx = jnp.clip(px, 0, fx_size - 1)
                cy = jnp.clip(py, 0, fy_size - 1)
                here = row16 == jy * 3 + jx
                start = lo_ref[k, cx, cy]
                span = len_ref[k, cx, cy] * inside.astype(jnp.int32)
                low = jnp.where(here, start, low)
                top = jnp.where(here, start + span, top)
        masks[pl.ds(own + k, 1)] = jnp.where(
            (lane >= low) & (lane < top), 1.0, 0.0).astype(BF16)[None]

    kern_copy = pltpu.make_async_remote_copy(
        kern.at[pl.ds(own, 3)], kern.at[pl.ds(own, 3)],
        v_send.at[3], v_recv.at[3], device_id=partner, device_id_type=MESH)
    mask_copy = pltpu.make_async_remote_copy(
        masks.at[pl.ds(own, 3)], masks.at[pl.ds(own, 3)],
        v_send.at[4], v_recv.at[4], device_id=partner, device_id_type=MESH)

    def img_copy(i):
        return pltpu.make_async_remote_copy(
            img_pack.at[i], img_got.at[i], v_send.at[i], v_recv.at[i],
            device_id=partner, device_id_type=MESH)

    kern_copy.start()
    mask_copy.start()

    low_half = lax.broadcasted_iota(jnp.int32, (64, 128), 1) < 64
    own_images.wait()
    for i in range(3):
        kept = jnp.broadcast_to(masks[own + i, 4:5, :].astype(F32), (64, 128)) > 0.5

        def fold(c, _, i=i, kept=kept):
            r = pl.multiple_of(c * 64, 64)
            first = jnp.where(kept, img_ref[i, pl.ds(r, 64), :].astype(F32), 0.0)
            second = jnp.where(kept, img_ref[i, pl.ds(r + 512, 64), :].astype(F32), 0.0)
            stay = jnp.where(low_half, first, second)
            move = jnp.where(low_half, second, first)
            img_pack[i, pl.ds(r, 64), :] = (stay + pltpu.roll(move, 64, 1)).astype(BF16)
            return 0

        lax.fori_loop(0, 8, fold, 0, unroll=2)
        img_copy(i).start()

    for d in DIRS:
        @pl.when(jnp.logical_not(exists(d)))
        def _(d=d):
            ref = landing(d)
            ref[...] = jnp.zeros(ref.shape, I16)
            got_scale[INDEX[d]] = jnp.zeros((8, 128), F32)

    kern_copy.wait()
    mask_copy.wait()

    zr = lax.broadcasted_iota(jnp.int32, (128, 128), 0)
    zc = lax.broadcasted_iota(jnp.int32, (128, 128), 1)
    near = (zc - zr <= 15) & (zr - zc <= 15)
    mz[...] = jnp.zeros_like(mz)

    def banded(row):
        return pltpu.roll(jnp.broadcast_to(row, (32, 128)), 1, 1, stride=1, stride_axis=0)

    lane32 = lax.broadcasted_iota(jnp.int32, (32, 128), 1)
    pos32 = lax.broadcasted_iota(jnp.int32, (32, 128), 0)

    def side_sums(row):
        taps = jnp.broadcast_to(row, (32, 128))
        before = jnp.sum(jnp.where(lane32 >= pos32 + 16, taps, 0.0), axis=1, keepdims=True)
        after = jnp.sum(jnp.where(lane32 <= pos32 - 17, taps, 0.0), axis=1, keepdims=True)
        middle = jnp.sum(
            jnp.where((lane32 < pos32 + 16) & (lane32 > pos32 - 17), taps, 0.0),
            axis=1, keepdims=True)
        return before, middle, after

    def tables(k, carry):
        sums_x, sums_y = carry
        rows = kern[k]
        near_x = rows[0:1].astype(BF16).astype(F32)
        near_y = rows[1:2].astype(BF16).astype(F32)
        near_z = rows[2:3].astype(BF16).astype(F32)
        gain = (jnp.sum(near_x, axis=1, keepdims=True)
                * jnp.sum(near_y, axis=1, keepdims=True)
                * jnp.sum(near_z, axis=1, keepdims=True))
        tx = banded(near_x)
        ty = banded(near_y)
        r = pl.multiple_of(k * 32, 32)
        fxt[pl.ds(r, 32), :] = tx.astype(BF16)
        fyt[k] = ty.astype(BF16)
        tpose[pl.ds(r, 32), :] = tx
        byt[k] = jnp.concatenate([ty, jnp.zeros((96, 128), F32)], axis=0).T[0:64, :].astype(BF16)
        tz = pltpu.roll(jnp.broadcast_to(near_z, (128, 128)), 113, 1, stride=1, stride_axis=0)
        tz = jnp.where(near, tz, 0.0)
        bzt[k] = tz.astype(BF16)
        fzt[k] = tz.T.astype(BF16)
        m = masks[k]
        mz[pl.ds(pl.multiple_of(k * 16, 16), 16), :] = dot(
            m, bzt[k]) / gain
        part = lane32 - k * 16
        mine = (part >= 0) & (part < 9)
        px = lax.rem(part + 96, 3)
        py = (part + 96) // 3 - 32
        for j, col in enumerate(side_sums(near_x)):
            sums_x = jnp.where(mine & (px == j), col, sums_x)
        for j, col in enumerate(side_sums(near_y)):
            sums_y = jnp.where(mine & (py == j), col, sums_y)
        return sums_x, sums_y

    zero = jnp.zeros((32, 128), F32)
    sums_x, sums_y = lax.fori_loop(0, 6, tables, (zero, zero))
    txs[...] = sums_x
    tys[...] = sums_y
    bxt[:, 0:128] = tpose[0:128, :].T[0:64].astype(BF16)
    bxt[:, 128:256] = tpose[128:256, :].T[0:64].astype(BF16)

    def weigh(q, _):
        parts = []
        for j in range(8):
            parts.append(txs[...] * tys[pl.ds(q * 8 + j, 1), :])
        w = jnp.dot(jnp.concatenate(parts, axis=0), mz[...],
                    preferred_element_type=F32, precision=lax.Precision.HIGHEST)
        low_inv[pl.ds(pl.multiple_of(q * 256, 256), 256), :] = 1.0 / (w + 0.5)
        return 0

    lax.fori_loop(0, 4, weigh, 0)

    def forward_y(k, p):
        cols = jnp.concatenate(
            [wide_a[pl.ds(k * 32 + p * 2 + j, 64, stride=PITCH_A), :].astype(BF16)
             for j in range(2)], axis=1)
        out = dot(fyt[k][:, 0:64], cols).astype(BF16)
        rows_u[p * 64:p * 64 + 32, :] = out[:, 0:128]
        rows_u[p * 64 + 32:p * 64 + 64, :] = out[:, 128:256]

    def backward_y(k, p):
        cols = jnp.concatenate(
            [rows_v[p * 64 + j * 32:p * 64 + j * 32 + 32, :] for j in range(2)], axis=1)
        out = dot(byt[k][:, 0:32], cols)
        for j in range(2):
            r = pl.multiple_of((k * 32 + p * 2 + j) * PITCH_B, 4)
            wide_b[pl.ds(r, 64), :] = out[:, j * 128:j * 128 + 128]

    def middle(k, images):
        covered = masks[k, 4:5, :].astype(F32) > 0.5
        for c in range(4):
            part = slice(c * 256, c * 256 + 256)
            f = dot(rows_u[part, :], fzt[k])
            pic = jnp.where(covered, images[part, :].astype(F32), 0.0)
            rows_r[part, :] = (pic / f).astype(BF16)
        for c in range(4):
            part = slice(c * 256, c * 256 + 256)
            rows_v[part, :] = dot(rows_r[part, :], bzt[k]).astype(BF16)

    def view_step(k, last, images):
        for p in range(16):
            forward_y(k, p)
            backward_y(last, p)
        middle(k, images)

    for step in range(ITERS):
        def pass_x(p, _):
            cols = jnp.concatenate([ext[p * 2], ext[p * 2 + 1]], axis=1)
            out = dot(fxt[:, 0:64], cols)
            for j in range(2):
                r = pl.multiple_of((p * 2 + j) * PITCH_A, 4)
                wide_a[pl.ds(r, 192), :] = out[:, j * 128:j * 128 + 128]
            return 0

        each(X_FACES, lambda d: recv_ext(ext_copy, d))
        lax.fori_loop(8, 24, pass_x, 0, unroll=8)
        each(NOT_X_FACES, lambda d: recv_ext(ext_copy, d))
        lax.fori_loop(0, 8, pass_x, 0, unroll=8)
        lax.fori_loop(24, 32, pass_x, 0, unroll=8)

        for p in range(16):
            forward_y(own, p)
        middle(own, img_ref.at[0])

        def own_views(n, _):
            view_step(own + n, own + n - 1, img_ref.at[n])
            return 0

        lax.fori_loop(1, 3, own_views, 0)

        if step == 0:
            for i in range(3):
                img_copy(i).wait()

                def unfold(c, _, i=i):
                    r = pl.multiple_of(c * 64, 64)
                    stay = img_got[i, pl.ds(r, 64), :].astype(F32)
                    move = pltpu.roll(stay, 64, 1)
                    img2[i, pl.ds(r, 64), :] = jnp.where(low_half, stay, move).astype(BF16)
                    img2[i, pl.ds(r + 512, 64), :] = jnp.where(low_half, move, stay).astype(BF16)
                    return 0

                lax.fori_loop(0, 8, unfold, 0, unroll=2)

        def other_views(n, _):
            view_step(oth + n, jnp.where(n == 0, own + 2, oth + n - 1), img2.at[n])
            return 0

        lax.fori_loop(0, 3, other_views, 0)
        for p in range(16):
            backward_y(oth + 2, p)

        def back_x(p, peak):
            pair = [wide_b[pl.ds(p * 2 + j, 192, stride=PITCH_B), :] for j in range(2)]
            hi, lo = split(jnp.concatenate(pair, axis=1))
            th = bxt[:, 0:192]
            out = dot(th, hi) + dot(th, lo)
            for j in range(2):
                part = out[:, j * 128:j * 128 + 128]
                corr[p * 2 + j] = part
                peak = jnp.maximum(peak, part)
            return peak

        def gain_of(peak, slot):
            peak = jnp.max(jnp.max(peak, axis=0, keepdims=True), axis=1, keepdims=True)
            peak = jnp.maximum(peak, 1e-30)
            scale[slot] = jnp.broadcast_to(peak * (1.0 / QMAX), (8, 128))
            return jnp.broadcast_to(QMAX / peak, (16, 128))

        def put(y, x, gain):
            quant[y, x:x + 16, :] = jnp.round(
                corr[y, x:x + 16, :] * gain).astype(jnp.int32).astype(I16)

        if step > 0:
            each(DIRS, lambda d: [c.wait_send() for c in corr_copies(d)])
        zeros = jnp.zeros((64, 128), F32)
        start = lambda d: [c.start() for c in corr_copies(d)]
        for slot, side in enumerate((core, 1 - core)):
            def back_side(p, peak, side=side):
                return back_x(side * 24 + p, peak)

            gain = gain_of(lax.fori_loop(0, 8, back_side, zeros, unroll=8), slot)

            def code_side(y, _, side=side, gain=gain):
                for x in (0, 16, 32, 48):
                    put(side * 48 + y, x, gain)
                return 0

            lax.fori_loop(0, 16, code_side, 0, unroll=4)
            toward(Y_FACES + CORNERS, 1 - slot, start)

        peak = lax.fori_loop(8, 24, back_x, zeros, unroll=8)
        inner = gain_of(peak, 2)

        def code_inner(y, _):
            put(y, 0, inner)
            put(y, 48, inner)
            return 0

        lax.fori_loop(16, 48, code_inner, 0, unroll=4)
        each(X_FACES, lambda d: [c.start() for c in corr_copies(d)])
        each(DIRS, lambda d: ext_copy(d).wait_send())
        each(DIRS, lambda d: recv_corr(corr_copies, d))

        factors = {d: jnp.broadcast_to(got_scale[INDEX[d], 0:1, :], (16, 128)) for d in DIRS}

        def wide(ref):
            return ref.astype(jnp.int32).astype(F32)

        def finish(y, i, sy):
            left = corr[y + 16, 16:32, :] + wide(got_x[0, y]) * factors[(0, -1)]
            right = corr[y + 16, 32:48, :] + wide(got_x[1, y]) * factors[(0, 1)]
            if sy:
                s = (sy + 1) // 2
                left = left + wide(got_y[s, i, 0:16]) * factors[(sy, 0)]
                left = left + wide(got_c[s, 0, i]) * factors[(sy, -1)]
                right = right + wide(got_y[s, i, 16:32]) * factors[(sy, 0)]
                right = right + wide(got_c[s, 1, i]) * factors[(sy, 1)]
            total = jnp.concatenate([left, right], axis=0)
            r = pl.multiple_of(y * 32, 32)
            new = joined[pl.ds(r, 32), :] * (total + 0.5) * low_inv[pl.ds(r, 32), :]
            if step + 1 < ITERS:
                joined[pl.ds(r, 32), :] = new
                ext[pl.ds(y + 16, 1), 16:48, :] = new.astype(BF16)[None]
            else:
                flat[pl.ds(y, 32, stride=40), :] = new

        def edges(i, _):
            finish(i, i, -1)
            finish(i + 17, i, 1)
            return 0

        lax.fori_loop(0, 15, edges, 0)
        finish(15, 0, 0)
        finish(16, 0, 0)
        if step + 1 < ITERS:
            send_ext()

    def put_out(x, _):
        out_ref[pl.ds(x * 4, 4)] = block[pl.ds(x * 4, 4), 0:32, :]
        return 0

    lax.fori_loop(0, 8, put_out, 0, unroll=2)
    each(DIRS, lambda d: [c.wait_send() for c in corr_copies(d)])


def recv_ext(copy, s):
    copy((-s[0], -s[1])).wait_recv()


def recv_corr(copies, s):
    for c in copies((-s[0], -s[1])):
        c.wait_recv()


def body(fx_size, fy_size, estimate, images, psf, cover_lo, cover_len):
    vmem = pl.BlockSpec(memory_space=pltpu.VMEM)
    smem = pl.BlockSpec(memory_space=pltpu.SMEM)
    anywhere = pl.BlockSpec(memory_space=pltpu.HBM)
    dma = pltpu.SemaphoreType.DMA
    out = pl.pallas_call(
        functools.partial(kernel, fx_size, fy_size),
        out_shape=jax.ShapeDtypeStruct((32, 32, 128), F32),
        in_specs=[anywhere, anywhere, vmem, smem, smem],
        out_specs=vmem,
        scratch_shapes=[
            pltpu.VMEM((32, 40, 128), F32),
            pltpu.VMEM((3, 1024, 128), BF16),
            pltpu.VMEM((3, 512, 128), BF16),
            pltpu.VMEM((3, 512, 128), BF16),
            pltpu.VMEM((64, 64, 128), BF16),
            pltpu.VMEM((1024, 128), F32),
            pltpu.VMEM((3, 1024, 128), BF16),
            pltpu.VMEM((6, 8, 128), F32),
            pltpu.VMEM((6, 16, 128), BF16),
            pltpu.VMEM((64 * PITCH_A, 128), F32),
            pltpu.VMEM((192 * PITCH_B, 128), F32),
            pltpu.VMEM((64, 64, 128), F32),
            pltpu.VMEM((64, 64, 128), I16),
            pltpu.VMEM((2, 32, 16, 128), I16),
            pltpu.VMEM((2, 15, 32, 128), I16),
            pltpu.VMEM((2, 2, 15, 16, 128), I16),
            pltpu.VMEM((3, 8, 128), F32),
            pltpu.VMEM((8, 8, 128), F32),
            pltpu.VMEM((192, 128), BF16),
            pltpu.VMEM((6, 32, 128), BF16),
            pltpu.VMEM((6, 128, 128), BF16),
            pltpu.VMEM((6, 128, 128), BF16),
            pltpu.VMEM((6, 64, 128), BF16),
            pltpu.VMEM((64, 256), BF16),
            pltpu.VMEM((1024, 128), F32),
            pltpu.VMEM((128, 128), F32),
            pltpu.VMEM((32, 128), F32),
            pltpu.VMEM((32, 128), F32),
            pltpu.VMEM((256, 128), F32),
            pltpu.VMEM((1024, 128), BF16),
            pltpu.VMEM((1024, 128), BF16),
            pltpu.VMEM((1024, 128), BF16),
            dma((8,)), dma((8,)), dma((8,)), dma((8,)),
            dma((8,)), dma((8,)), dma((5,)), dma((5,)), dma((2,)),
        ],
        compiler_params=pltpu.CompilerParams(
            collective_id=0, has_side_effects=True, vmem_limit_bytes=40 << 20),
    )(
        *(pltpu.with_memory_space_constraint(a, pltpu.HBM) for a in (
            estimate, images.reshape(3, 1024, 128), psf, cover_lo, cover_len)))
    return out


def solution(mesh):
    return jax.shard_map(
        functools.partial(body, mesh.shape["fx"], mesh.shape["fy"]),
        mesh=mesh,
        in_specs=(
            P("fx", "fy", None),
            P("view", "fx", "fy", None),
            P("view", None, None),
            P("view", None, None),
            P("view", None, None),
        ),
        out_specs=P("fx", "fy", None),
        check_vma=False,
    )
```

```python
import functools

import jax
import jax.numpy as jnp
from jax import lax
from jax.experimental import pallas as pl
from jax.experimental.pallas import tpu as pltpu
from jax.sharding import PartitionSpec as P

ITERS = 2
MESH = pl.DeviceIdType.MESH
BF16 = jnp.bfloat16
F32 = jnp.float32
I16 = jnp.int16
QMAX = 32000.0
PITCH_A = 196
PITCH_B = 68

DIRS = tuple((dy, dx) for dy in (-1, 0, 1) for dx in (-1, 0, 1) if dy or dx)
INDEX = {d: i for i, d in enumerate(DIRS)}
X_FACES = ((0, 1), (0, -1))
NOT_X_FACES = ((1, 0), (-1, 0), (1, 1), (1, -1), (-1, 1), (-1, -1))
Y_FACES = NOT_X_FACES[:2]
CORNERS = NOT_X_FACES[2:]

E_SRC_Y = {1: (33, 15), -1: (16, 15), 0: (16, 32)}
E_DST_Y = {-1: (1, 15), 1: (48, 15), 0: (16, 32)}
E_SRC_X = {1: (32, 16), -1: (16, 16), 0: (16, 32)}
E_DST_X = {-1: (0, 16), 1: (48, 16), 0: (16, 32)}
C_SRC_Y = {1: (48, 15), -1: (1, 15), 0: (16, 32)}
C_SRC_X = {1: (48, 16), -1: (0, 16), 0: (16, 32)}


def dot(a, b):
    return jnp.dot(a, b, preferred_element_type=F32)


def split(v):
    hi = v.astype(BF16)
    return hi, (v - hi.astype(F32)).astype(BF16)


def kernel(
    fx_size, fy_size,
    est_any, img_any, psf_ref, lo_ref, len_ref, out_ref,
    block, img_ref, img_pack, img_got,
    ext, joined, img2, kern, masks, wide_a, wide_b, corr, quant,
    got_x, got_y, got_c, scale, got_scale,
    fxt, fyt, fzt, bzt, byt, bxt, low_inv, mz, txs, tys, tpose, rows_u, rows_r, rows_v,
    e_send, e_recv, c_send, c_recv, s_send, s_recv, v_send, v_recv, own_sem,
):
    g = lax.axis_index("view")
    bx = lax.axis_index("fx")
    by = lax.axis_index("fy")
    core = lax.rem(by, 2)
    own = g * 3
    oth = 3 - own

    def exists(d):
        dy, dx = d
        ok = jnp.bool_(True)
        if dy:
            ok = ok & (by + dy >= 0) & (by + dy < fy_size)
        if dx:
            ok = ok & (bx + dx >= 0) & (bx + dx < fx_size)
        return ok

    def peer(d):
        dy, dx = d
        cross = core if dy == 1 else (1 - core if dy == -1 else 0)
        return (g + cross - 2 * g * cross, bx + dx, by + dy)

    partner = (1 - g, bx, by)

    def ext_copy(d):
        s = (-d[0], -d[1])
        ys, ny = E_SRC_Y[d[0]]
        xs, nx = E_SRC_X[d[1]]
        yd, _ = E_DST_Y[s[0]]
        xd, _ = E_DST_X[s[1]]
        return pltpu.make_async_remote_copy(
            ext.at[pl.ds(ys, ny), pl.ds(xs, nx), :],
            ext.at[pl.ds(yd, ny), pl.ds(xd, nx), :],
            e_send.at[INDEX[d]], e_recv.at[INDEX[s]],
            device_id=peer(d), device_id_type=MESH)

    def landing(s):
        if s[0] == 0:
            return got_x.at[(s[1] + 1) // 2]
        if s[1] == 0:
            return got_y.at[(s[0] + 1) // 2]
        return got_c.at[(s[0] + 1) // 2, (s[1] + 1) // 2]

    def corr_copies(d):
        s = (-d[0], -d[1])
        ys, ny = C_SRC_Y[d[0]]
        xs, nx = C_SRC_X[d[1]]
        return (
            pltpu.make_async_remote_copy(
                scale.at[1 - leaving(d) if d[0] else 2], got_scale.at[INDEX[s]],
                s_send.at[INDEX[d]], s_recv.at[INDEX[s]],
                device_id=peer(d), device_id_type=MESH),
            pltpu.make_async_remote_copy(
                quant.at[pl.ds(ys, ny), pl.ds(xs, nx), :], landing(s),
                c_send.at[INDEX[d]], c_recv.at[INDEX[s]],
                device_id=peer(d), device_id_type=MESH),
        )

    def each(order, action):
        for d in order:
            @pl.when(exists(d))
            def _(d=d):
                action(d)

    def leaving(d):
        return core if d[0] == 1 else 1 - core

    def toward(order, out, action):
        for d in order:
            @pl.when(exists(d) & (leaving(d) == out))
            def _(d=d):
                action(d)

    def send_ext():
        start = lambda d: ext_copy(d).start()
        each(Y_FACES, start)
        toward(CORNERS, 1, start)
        each(X_FACES, start)
        toward(CORNERS, 0, start)

    est_copy = pltpu.make_async_copy(est_any, block.at[:, 0:32, :], own_sem.at[0])
    est_copy.start()
    own_images = pltpu.make_async_copy(img_any, img_ref, own_sem.at[1])
    own_images.start()
    kern[...] = jnp.zeros_like(kern)
    ext[...] = jnp.zeros_like(ext)

    barrier = pltpu.get_barrier_semaphore()
    count = jnp.int32(1)
    for d in DIRS:
        count = count + exists(d).astype(jnp.int32)
    pl.semaphore_signal(barrier, inc=1, device_id=partner, device_id_type=MESH)
    each(DIRS, lambda d: pl.semaphore_signal(
        barrier, inc=1, device_id=peer(d), device_id_type=MESH))


    flat = block.reshape(32 * 40, 128)
    est_copy.wait()

    def load_est(y, _):
        row = flat[pl.ds(y, 32, stride=40), :]
        joined[pl.ds(pl.multiple_of(y * 32, 32), 32), :] = row
        ext[pl.ds(y + 16, 1), 16:48, :] = row.astype(BF16)[None]
        return 0

    lax.fori_loop(0, 32, load_est, 0, unroll=4)

    pl.semaphore_wait(barrier, count)
    send_ext()

    lane = lax.broadcasted_iota(jnp.int32, (16, 128), 1)
    row16 = lax.broadcasted_iota(jnp.int32, (16, 128), 0)
    for k in range(3):
        taps = psf_ref[k]
        kern[pl.ds(own + k, 1), 0:3, 0:31] = (taps / jnp.sum(taps, axis=-1, keepdims=True))[None]
        low = jnp.zeros((16, 128), jnp.int32)
        top = jnp.zeros((16, 128), jnp.int32)
        for jy in range(3):
            for jx in range(3):
                px = bx + (jx - 1)
                py = by + (jy - 1)
                inside = (px >= 0) & (px < fx_size) & (py >= 0) & (py < fy_size)
                cx = jnp.clip(px, 0, fx_size - 1)
                cy = jnp.clip(py, 0, fy_size - 1)
                here = row16 == jy * 3 + jx
                start = lo_ref[k, cx, cy]
                span = len_ref[k, cx, cy] * inside.astype(jnp.int32)
                low = jnp.where(here, start, low)
                top = jnp.where(here, start + span, top)
        masks[pl.ds(own + k, 1)] = jnp.where(
            (lane >= low) & (lane < top), 1.0, 0.0).astype(BF16)[None]

    kern_copy = pltpu.make_async_remote_copy(
        kern.at[pl.ds(own, 3)], kern.at[pl.ds(own, 3)],
        v_send.at[3], v_recv.at[3], device_id=partner, device_id_type=MESH)
    mask_copy = pltpu.make_async_remote_copy(
        masks.at[pl.ds(own, 3)], masks.at[pl.ds(own, 3)],
        v_send.at[4], v_recv.at[4], device_id=partner, device_id_type=MESH)

    def img_copy(i):
        return pltpu.make_async_remote_copy(
            img_pack.at[i], img_got.at[i], v_send.at[i], v_recv.at[i],
            device_id=partner, device_id_type=MESH)

    kern_copy.start()
    mask_copy.start()

    low_half = lax.broadcasted_iota(jnp.int32, (64, 128), 1) < 64
    own_images.wait()
    for i in range(3):
        kept = jnp.broadcast_to(masks[own + i, 4:5, :].astype(F32), (64, 128)) > 0.5

        def fold(c, _, i=i, kept=kept):
            r = pl.multiple_of(c * 64, 64)
            first = jnp.where(kept, img_ref[i, pl.ds(r, 64), :].astype(F32), 0.0)
            second = jnp.where(kept, img_ref[i, pl.ds(r + 512, 64), :].astype(F32), 0.0)
            stay = jnp.where(low_half, first, second)
            move = jnp.where(low_half, second, first)
            img_pack[i, pl.ds(r, 64), :] = (stay + pltpu.roll(move, 64, 1)).astype(BF16)
            return 0

        lax.fori_loop(0, 8, fold, 0, unroll=2)
        img_copy(i).start()

    for d in DIRS:
        @pl.when(jnp.logical_not(exists(d)))
        def _(d=d):
            ref = landing(d)
            ref[...] = jnp.zeros(ref.shape, I16)
            got_scale[INDEX[d]] = jnp.zeros((8, 128), F32)

    kern_copy.wait()
    mask_copy.wait()

    zr = lax.broadcasted_iota(jnp.int32, (128, 128), 0)
    zc = lax.broadcasted_iota(jnp.int32, (128, 128), 1)
    near = (zc - zr <= 15) & (zr - zc <= 15)
    mz[...] = jnp.zeros_like(mz)

    def banded(row):
        return pltpu.roll(jnp.broadcast_to(row, (32, 128)), 1, 1, stride=1, stride_axis=0)

    lane32 = lax.broadcasted_iota(jnp.int32, (32, 128), 1)
    pos32 = lax.broadcasted_iota(jnp.int32, (32, 128), 0)

    def side_sums(row):
        taps = jnp.broadcast_to(row, (32, 128))
        before = jnp.sum(jnp.where(lane32 >= pos32 + 16, taps, 0.0), axis=1, keepdims=True)
        after = jnp.sum(jnp.where(lane32 <= pos32 - 17, taps, 0.0), axis=1, keepdims=True)
        middle = jnp.sum(
            jnp.where((lane32 < pos32 + 16) & (lane32 > pos32 - 17), taps, 0.0),
            axis=1, keepdims=True)
        return before, middle, after

    def tables(k, carry):
        sums_x, sums_y = carry
        rows = kern[k]
        near_x = rows[0:1].astype(BF16).astype(F32)
        near_y = rows[1:2].astype(BF16).astype(F32)
        near_z = rows[2:3].astype(BF16).astype(F32)
        gain = (jnp.sum(near_x, axis=1, keepdims=True)
                * jnp.sum(near_y, axis=1, keepdims=True)
                * jnp.sum(near_z, axis=1, keepdims=True))
        tx = banded(near_x)
        ty = banded(near_y)
        r = pl.multiple_of(k * 32, 32)
        fxt[pl.ds(r, 32), :] = tx.astype(BF16)
        fyt[k] = ty.astype(BF16)
        tpose[pl.ds(r, 32), :] = tx
        byt[k] = jnp.concatenate([ty, jnp.zeros((96, 128), F32)], axis=0).T[0:64, :].astype(BF16)
        tz = pltpu.roll(jnp.broadcast_to(near_z, (128, 128)), 113, 1, stride=1, stride_axis=0)
        tz = jnp.where(near, tz, 0.0)
        bzt[k] = tz.astype(BF16)
        fzt[k] = tz.T.astype(BF16)
        m = masks[k]
        mz[pl.ds(pl.multiple_of(k * 16, 16), 16), :] = dot(
            m, bzt[k]) / gain
        part = lane32 - k * 16
        mine = (part >= 0) & (part < 9)
        px = lax.rem(part + 96, 3)
        py = (part + 96) // 3 - 32
        for j, col in enumerate(side_sums(near_x)):
            sums_x = jnp.where(mine & (px == j), col, sums_x)
        for j, col in enumerate(side_sums(near_y)):
            sums_y = jnp.where(mine & (py == j), col, sums_y)
        return sums_x, sums_y

    zero = jnp.zeros((32, 128), F32)
    sums_x, sums_y = lax.fori_loop(0, 6, tables, (zero, zero))
    txs[...] = sums_x
    tys[...] = sums_y
    bxt[:, 0:128] = tpose[0:128, :].T[0:64].astype(BF16)
    bxt[:, 128:256] = tpose[128:256, :].T[0:64].astype(BF16)

    def weigh(q, _):
        parts = []
        for j in range(8):
            parts.append(txs[...] * tys[pl.ds(q * 8 + j, 1), :])
        w = jnp.dot(jnp.concatenate(parts, axis=0), mz[...],
                    preferred_element_type=F32, precision=lax.Precision.HIGHEST)
        low_inv[pl.ds(pl.multiple_of(q * 256, 256), 256), :] = 1.0 / (w + 0.5)
        return 0

    lax.fori_loop(0, 4, weigh, 0)

    def forward_y(k, p):
        cols = jnp.concatenate(
            [wide_a[pl.ds(k * 32 + p * 2 + j, 64, stride=PITCH_A), :].astype(BF16)
             for j in range(2)], axis=1)
        out = dot(fyt[k][:, 0:64], cols).astype(BF16)
        rows_u[p * 64:p * 64 + 32, :] = out[:, 0:128]
        rows_u[p * 64 + 32:p * 64 + 64, :] = out[:, 128:256]

    def backward_y(k, p):
        cols = jnp.concatenate(
            [rows_v[p * 64 + j * 32:p * 64 + j * 32 + 32, :] for j in range(2)], axis=1)
        out = dot(byt[k][:, 0:32], cols)
        for j in range(2):
            r = pl.multiple_of((k * 32 + p * 2 + j) * PITCH_B, 4)
            wide_b[pl.ds(r, 64), :] = out[:, j * 128:j * 128 + 128]

    def middle(k, images):
        covered = masks[k, 4:5, :].astype(F32) > 0.5
        for c in range(4):
            part = slice(c * 256, c * 256 + 256)
            f = dot(rows_u[part, :], fzt[k])
            pic = jnp.where(covered, images[part, :].astype(F32), 0.0)
            rows_r[part, :] = (pic / f).astype(BF16)
        for c in range(4):
            part = slice(c * 256, c * 256 + 256)
            rows_v[part, :] = dot(rows_r[part, :], bzt[k]).astype(BF16)

    def view_step(k, last, images):
        for p in range(16):
            forward_y(k, p)
            backward_y(last, p)
        middle(k, images)

    for step in range(ITERS):
        def pass_x(p, _):
            cols = jnp.concatenate([ext[p * 2], ext[p * 2 + 1]], axis=1)
            out = dot(fxt[:, 0:64], cols)
            for j in range(2):
                r = pl.multiple_of((p * 2 + j) * PITCH_A, 4)
                wide_a[pl.ds(r, 192), :] = out[:, j * 128:j * 128 + 128]
            return 0

        each(X_FACES, lambda d: recv_ext(ext_copy, d))
        lax.fori_loop(8, 24, pass_x, 0, unroll=8)
        for out, side in enumerate((1 - core, core)):
            toward(NOT_X_FACES, out, lambda d: recv_ext(ext_copy, d))
            lax.fori_loop(0, 8, lambda p, c, side=side: pass_x(side * 24 + p, c), 0, unroll=8)

        for p in range(16):
            forward_y(own, p)
        middle(own, img_ref.at[0])

        def own_views(n, _):
            view_step(own + n, own + n - 1, img_ref.at[n])
            return 0

        lax.fori_loop(1, 3, own_views, 0)

        if step == 0:
            for i in range(3):
                img_copy(i).wait()

                def unfold(c, _, i=i):
                    r = pl.multiple_of(c * 64, 64)
                    stay = img_got[i, pl.ds(r, 64), :].astype(F32)
                    move = pltpu.roll(stay, 64, 1)
                    img2[i, pl.ds(r, 64), :] = jnp.where(low_half, stay, move).astype(BF16)
                    img2[i, pl.ds(r + 512, 64), :] = jnp.where(low_half, move, stay).astype(BF16)
                    return 0

                lax.fori_loop(0, 8, unfold, 0, unroll=2)

        def other_views(n, _):
            view_step(oth + n, jnp.where(n == 0, own + 2, oth + n - 1), img2.at[n])
            return 0

        lax.fori_loop(0, 3, other_views, 0)
        for p in range(16):
            backward_y(oth + 2, p)

        def back_x(p, peak):
            pair = [wide_b[pl.ds(p * 2 + j, 192, stride=PITCH_B), :] for j in range(2)]
            hi, lo = split(jnp.concatenate(pair, axis=1))
            th = bxt[:, 0:192]
            out = dot(th, hi) + dot(th, lo)
            for j in range(2):
                part = out[:, j * 128:j * 128 + 128]
                corr[p * 2 + j] = part
                peak = jnp.maximum(peak, part)
            return peak

        def gain_of(peak, slot):
            peak = jnp.max(jnp.max(peak, axis=0, keepdims=True), axis=1, keepdims=True)
            peak = jnp.maximum(peak, 1e-30)
            scale[slot] = jnp.broadcast_to(peak * (1.0 / QMAX), (8, 128))
            return jnp.broadcast_to(QMAX / peak, (16, 128))

        def put(y, x, gain):
            quant[y, x:x + 16, :] = jnp.round(
                corr[y, x:x + 16, :] * gain).astype(jnp.int32).astype(I16)

        if step > 0:
            each(DIRS, lambda d: [c.wait_send() for c in corr_copies(d)])
        zeros = jnp.zeros((64, 128), F32)
        start = lambda d: [c.start() for c in corr_copies(d)]
        for slot, side in enumerate((core, 1 - core)):
            def back_side(p, peak, side=side):
                return back_x(side * 24 + p, peak)

            gain = gain_of(lax.fori_loop(0, 8, back_side, zeros, unroll=8), slot)

            def code_side(y, _, side=side, gain=gain):
                for x in (0, 16, 32, 48):
                    put(side * 48 + y, x, gain)
                return 0

            lax.fori_loop(0, 16, code_side, 0, unroll=4)
            toward(Y_FACES + CORNERS, 1 - slot, start)

        peak = lax.fori_loop(8, 24, back_x, zeros, unroll=8)
        inner = gain_of(peak, 2)

        def code_inner(y, _):
            put(y, 0, inner)
            put(y, 48, inner)
            return 0

        lax.fori_loop(16, 48, code_inner, 0, unroll=4)
        each(X_FACES, lambda d: [c.start() for c in corr_copies(d)])
        each(DIRS, lambda d: ext_copy(d).wait_send())
        each(X_FACES, lambda d: recv_corr(corr_copies, d))

        def factor(index):
            return jnp.broadcast_to(got_scale[index, 0:1, :], (16, 128))

        from_low, from_high = factor(INDEX[(0, -1)]), factor(INDEX[(0, 1)])

        def wide(ref):
            return ref.astype(jnp.int32).astype(F32)

        def finish(y, i=None, s=None, near=None):
            left = corr[y + 16, 16:32, :] + wide(got_x[0, y]) * from_low
            right = corr[y + 16, 32:48, :] + wide(got_x[1, y]) * from_high
            if near is not None:
                left = left + wide(got_y[s, i, 0:16]) * near[1]
                left = left + wide(got_c[s, 0, i]) * near[0]
                right = right + wide(got_y[s, i, 16:32]) * near[1]
                right = right + wide(got_c[s, 1, i]) * near[2]
            total = jnp.concatenate([left, right], axis=0)
            r = pl.multiple_of(y * 32, 32)
            new = joined[pl.ds(r, 32), :] * (total + 0.5) * low_inv[pl.ds(r, 32), :]
            if step + 1 < ITERS:
                joined[pl.ds(r, 32), :] = new
                ext[pl.ds(y + 16, 1), 16:48, :] = new.astype(BF16)[None]
            else:
                flat[pl.ds(y, 32, stride=40), :] = new

        finish(15)
        finish(16)
        for out, side in enumerate((1 - core, core)):
            toward(NOT_X_FACES, out, lambda d: recv_corr(corr_copies, d))
            near = [factor(side * 5 + j) for j in range(3)]

            def edges(i, _, side=side, near=near):
                finish(i + 17 * side, i, side, near)
                return 0

            lax.fori_loop(0, 15, edges, 0, unroll=3)
        if step + 1 < ITERS:
            send_ext()

    def put_out(x, _):
        out_ref[pl.ds(x * 4, 4)] = block[pl.ds(x * 4, 4), 0:32, :]
        return 0

    lax.fori_loop(0, 8, put_out, 0, unroll=2)
    each(DIRS, lambda d: [c.wait_send() for c in corr_copies(d)])


def recv_ext(copy, s):
    copy((-s[0], -s[1])).wait_recv()


def recv_corr(copies, s):
    for c in copies((-s[0], -s[1])):
        c.wait_recv()


def body(fx_size, fy_size, estimate, images, psf, cover_lo, cover_len):
    vmem = pl.BlockSpec(memory_space=pltpu.VMEM)
    smem = pl.BlockSpec(memory_space=pltpu.SMEM)
    anywhere = pl.BlockSpec(memory_space=pltpu.HBM)
    dma = pltpu.SemaphoreType.DMA
    out = pl.pallas_call(
        functools.partial(kernel, fx_size, fy_size),
        out_shape=jax.ShapeDtypeStruct((32, 32, 128), F32),
        in_specs=[anywhere, anywhere, vmem, smem, smem],
        out_specs=vmem,
        scratch_shapes=[
            pltpu.VMEM((32, 40, 128), F32),
            pltpu.VMEM((3, 1024, 128), BF16),
            pltpu.VMEM((3, 512, 128), BF16),
            pltpu.VMEM((3, 512, 128), BF16),
            pltpu.VMEM((64, 64, 128), BF16),
            pltpu.VMEM((1024, 128), F32),
            pltpu.VMEM((3, 1024, 128), BF16),
            pltpu.VMEM((6, 8, 128), F32),
            pltpu.VMEM((6, 16, 128), BF16),
            pltpu.VMEM((64 * PITCH_A, 128), F32),
            pltpu.VMEM((192 * PITCH_B, 128), F32),
            pltpu.VMEM((64, 64, 128), F32),
            pltpu.VMEM((64, 64, 128), I16),
            pltpu.VMEM((2, 32, 16, 128), I16),
            pltpu.VMEM((2, 15, 32, 128), I16),
            pltpu.VMEM((2, 2, 15, 16, 128), I16),
            pltpu.VMEM((3, 8, 128), F32),
            pltpu.VMEM((8, 8, 128), F32),
            pltpu.VMEM((192, 128), BF16),
            pltpu.VMEM((6, 32, 128), BF16),
            pltpu.VMEM((6, 128, 128), BF16),
            pltpu.VMEM((6, 128, 128), BF16),
            pltpu.VMEM((6, 64, 128), BF16),
            pltpu.VMEM((64, 256), BF16),
            pltpu.VMEM((1024, 128), F32),
            pltpu.VMEM((128, 128), F32),
            pltpu.VMEM((32, 128), F32),
            pltpu.VMEM((32, 128), F32),
            pltpu.VMEM((256, 128), F32),
            pltpu.VMEM((1024, 128), BF16),
            pltpu.VMEM((1024, 128), BF16),
            pltpu.VMEM((1024, 128), BF16),
            dma((8,)), dma((8,)), dma((8,)), dma((8,)),
            dma((8,)), dma((8,)), dma((5,)), dma((5,)), dma((2,)),
        ],
        compiler_params=pltpu.CompilerParams(
            collective_id=0, has_side_effects=True, vmem_limit_bytes=40 << 20),
    )(
        *(pltpu.with_memory_space_constraint(a, pltpu.HBM) for a in (
            estimate, images.reshape(3, 1024, 128), psf, cover_lo, cover_len)))
    return out


def solution(mesh):
    return jax.shard_map(
        functools.partial(body, mesh.shape["fx"], mesh.shape["fy"]),
        mesh=mesh,
        in_specs=(
            P("fx", "fy", None),
            P("view", "fx", "fy", None),
            P("view", None, None),
            P("view", None, None),
            P("view", None, None),
        ),
        out_specs=P("fx", "fy", None),
        check_vma=False,
    )
```

```python
import functools

import jax
import jax.numpy as jnp
from jax import lax
from jax.experimental import pallas as pl
from jax.experimental.pallas import tpu as pltpu
from jax.sharding import PartitionSpec as P

ITERS = 2
MESH = pl.DeviceIdType.MESH
BF16 = jnp.bfloat16
F32 = jnp.float32
I16 = jnp.int16
QMAX = 32000.0
PITCH_A = 196
PITCH_B = 68

DIRS = tuple((dy, dx) for dy in (-1, 0, 1) for dx in (-1, 0, 1) if dy or dx)
INDEX = {d: i for i, d in enumerate(DIRS)}
X_FACES = ((0, 1), (0, -1))
NOT_X_FACES = ((1, 0), (-1, 0), (1, 1), (1, -1), (-1, 1), (-1, -1))
Y_FACES = NOT_X_FACES[:2]
CORNERS = NOT_X_FACES[2:]

E_SRC_Y = {1: (33, 15), -1: (16, 15), 0: (16, 32)}
E_DST_Y = {-1: (1, 15), 1: (48, 15), 0: (16, 32)}
E_SRC_X = {1: (32, 16), -1: (16, 16), 0: (16, 32)}
E_DST_X = {-1: (0, 16), 1: (48, 16), 0: (16, 32)}
C_SRC_Y = {1: (48, 15), -1: (1, 15), 0: (16, 32)}
C_SRC_X = {1: (48, 16), -1: (0, 16), 0: (16, 32)}


def dot(a, b):
    return jnp.dot(a, b, preferred_element_type=F32)


def split(v):
    hi = v.astype(BF16)
    return hi, (v - hi.astype(F32)).astype(BF16)


def kernel(
    fx_size, fy_size,
    est_any, img_any, psf_ref, lo_ref, len_ref, out_ref,
    block, img_ref, img_pack, img_got,
    ext, joined, img2, kern, masks, wide_a, wide_b, corr, quant,
    got_x, got_y, got_c, scale, got_scale,
    fxt, fyt, fzt, bzt, byt, bxt, low_inv, mz, txs, tys, tpose, rows_u, rows_r, rows_v,
    e_send, e_recv, c_send, c_recv, s_send, s_recv, v_send, v_recv, own_sem,
):
    g = lax.axis_index("view")
    bx = lax.axis_index("fx")
    by = lax.axis_index("fy")
    core = lax.rem(by, 2)
    own = g * 3
    oth = 3 - own

    def exists(d):
        dy, dx = d
        ok = jnp.bool_(True)
        if dy:
            ok = ok & (by + dy >= 0) & (by + dy < fy_size)
        if dx:
            ok = ok & (bx + dx >= 0) & (bx + dx < fx_size)
        return ok

    def peer(d):
        dy, dx = d
        cross = core if dy == 1 else (1 - core if dy == -1 else 0)
        return (g + cross - 2 * g * cross, bx + dx, by + dy)

    partner = (1 - g, bx, by)

    def ext_copy(d):
        s = (-d[0], -d[1])
        ys, ny = E_SRC_Y[d[0]]
        xs, nx = E_SRC_X[d[1]]
        yd, _ = E_DST_Y[s[0]]
        xd, _ = E_DST_X[s[1]]
        return pltpu.make_async_remote_copy(
            ext.at[pl.ds(ys, ny), pl.ds(xs, nx), :],
            ext.at[pl.ds(yd, ny), pl.ds(xd, nx), :],
            e_send.at[INDEX[d]], e_recv.at[INDEX[s]],
            device_id=peer(d), device_id_type=MESH)

    def landing(s):
        if s[0] == 0:
            return got_x.at[(s[1] + 1) // 2]
        if s[1] == 0:
            return got_y.at[(s[0] + 1) // 2]
        return got_c.at[(s[0] + 1) // 2, (s[1] + 1) // 2]

    def corr_copies(d):
        s = (-d[0], -d[1])
        ys, ny = C_SRC_Y[d[0]]
        xs, nx = C_SRC_X[d[1]]
        return (
            pltpu.make_async_remote_copy(
                scale.at[1 - leaving(d) if d[0] else 2], got_scale.at[INDEX[s]],
                s_send.at[INDEX[d]], s_recv.at[INDEX[s]],
                device_id=peer(d), device_id_type=MESH),
            pltpu.make_async_remote_copy(
                quant.at[pl.ds(ys, ny), pl.ds(xs, nx), :], landing(s),
                c_send.at[INDEX[d]], c_recv.at[INDEX[s]],
                device_id=peer(d), device_id_type=MESH),
        )

    def each(order, action):
        for d in order:
            @pl.when(exists(d))
            def _(d=d):
                action(d)

    def leaving(d):
        return core if d[0] == 1 else 1 - core

    def toward(order, out, action):
        for d in order:
            @pl.when(exists(d) & (leaving(d) == out))
            def _(d=d):
                action(d)

    def send_ext():
        start = lambda d: ext_copy(d).start()
        each(Y_FACES, start)
        toward(CORNERS, 1, start)
        each(X_FACES, start)
        toward(CORNERS, 0, start)

    est_copy = pltpu.make_async_copy(est_any, block.at[:, 0:32, :], own_sem.at[0])
    est_copy.start()
    own_images = pltpu.make_async_copy(img_any, img_ref, own_sem.at[1])
    own_images.start()
    kern[...] = jnp.zeros_like(kern)
    ext[...] = jnp.zeros_like(ext)

    barrier = pltpu.get_barrier_semaphore()
    count = jnp.int32(1)
    for d in DIRS:
        count = count + exists(d).astype(jnp.int32)
    pl.semaphore_signal(barrier, inc=1, device_id=partner, device_id_type=MESH)
    each(DIRS, lambda d: pl.semaphore_signal(
        barrier, inc=1, device_id=peer(d), device_id_type=MESH))


    flat = block.reshape(32 * 40, 128)
    est_copy.wait()

    def load_est(y, _):
        row = flat[pl.ds(y, 32, stride=40), :]
        joined[pl.ds(pl.multiple_of(y * 32, 32), 32), :] = row
        ext[pl.ds(y + 16, 1), 16:48, :] = row.astype(BF16)[None]
        return 0

    lax.fori_loop(0, 32, load_est, 0, unroll=4)

    pl.semaphore_wait(barrier, count)
    send_ext()

    lane = lax.broadcasted_iota(jnp.int32, (16, 128), 1)
    row16 = lax.broadcasted_iota(jnp.int32, (16, 128), 0)
    for k in range(3):
        taps = psf_ref[k]
        kern[pl.ds(own + k, 1), 0:3, 0:31] = (taps / jnp.sum(taps, axis=-1, keepdims=True))[None]
        low = jnp.zeros((16, 128), jnp.int32)
        top = jnp.zeros((16, 128), jnp.int32)
        for jy in range(3):
            for jx in range(3):
                px = bx + (jx - 1)
                py = by + (jy - 1)
                inside = (px >= 0) & (px < fx_size) & (py >= 0) & (py < fy_size)
                cx = jnp.clip(px, 0, fx_size - 1)
                cy = jnp.clip(py, 0, fy_size - 1)
                here = row16 == jy * 3 + jx
                start = lo_ref[k, cx, cy]
                span = len_ref[k, cx, cy] * inside.astype(jnp.int32)
                low = jnp.where(here, start, low)
                top = jnp.where(here, start + span, top)
        masks[pl.ds(own + k, 1)] = jnp.where(
            (lane >= low) & (lane < top), 1.0, 0.0).astype(BF16)[None]

    kern_copy = pltpu.make_async_remote_copy(
        kern.at[pl.ds(own, 3)], kern.at[pl.ds(own, 3)],
        v_send.at[3], v_recv.at[3], device_id=partner, device_id_type=MESH)
    mask_copy = pltpu.make_async_remote_copy(
        masks.at[pl.ds(own, 3)], masks.at[pl.ds(own, 3)],
        v_send.at[4], v_recv.at[4], device_id=partner, device_id_type=MESH)

    def img_copy(i):
        return pltpu.make_async_remote_copy(
            img_pack.at[i], img_got.at[i], v_send.at[i], v_recv.at[i],
            device_id=partner, device_id_type=MESH)

    kern_copy.start()
    mask_copy.start()

    low_half = lax.broadcasted_iota(jnp.int32, (64, 128), 1) < 64
    own_images.wait()
    for i in range(3):
        kept = jnp.broadcast_to(masks[own + i, 4:5, :].astype(F32), (64, 128)) > 0.5

        def fold(c, _, i=i, kept=kept):
            r = pl.multiple_of(c * 64, 64)
            first = jnp.where(kept, img_ref[i, pl.ds(r, 64), :].astype(F32), 0.0)
            second = jnp.where(kept, img_ref[i, pl.ds(r + 512, 64), :].astype(F32), 0.0)
            stay = jnp.where(low_half, first, second)
            move = jnp.where(low_half, second, first)
            img_pack[i, pl.ds(r, 64), :] = (stay + pltpu.roll(move, 64, 1)).astype(BF16)
            return 0

        lax.fori_loop(0, 8, fold, 0, unroll=2)
        img_copy(i).start()

    for d in DIRS:
        @pl.when(jnp.logical_not(exists(d)))
        def _(d=d):
            ref = landing(d)
            ref[...] = jnp.zeros(ref.shape, I16)
            got_scale[INDEX[d]] = jnp.zeros((8, 128), F32)

    kern_copy.wait()
    mask_copy.wait()

    zr = lax.broadcasted_iota(jnp.int32, (128, 128), 0)
    zc = lax.broadcasted_iota(jnp.int32, (128, 128), 1)
    near = (zc - zr <= 15) & (zr - zc <= 15)
    mz[...] = jnp.zeros_like(mz)

    def banded(row):
        return pltpu.roll(jnp.broadcast_to(row, (32, 128)), 1, 1, stride=1, stride_axis=0)

    lane32 = lax.broadcasted_iota(jnp.int32, (32, 128), 1)
    pos32 = lax.broadcasted_iota(jnp.int32, (32, 128), 0)

    def side_sums(row):
        taps = jnp.broadcast_to(row, (32, 128))
        before = jnp.sum(jnp.where(lane32 >= pos32 + 16, taps, 0.0), axis=1, keepdims=True)
        after = jnp.sum(jnp.where(lane32 <= pos32 - 17, taps, 0.0), axis=1, keepdims=True)
        middle = jnp.sum(
            jnp.where((lane32 < pos32 + 16) & (lane32 > pos32 - 17), taps, 0.0),
            axis=1, keepdims=True)
        return before, middle, after

    def tables(k, carry):
        sums_x, sums_y = carry
        rows = kern[k]
        near_x = rows[0:1].astype(BF16).astype(F32)
        near_y = rows[1:2].astype(BF16).astype(F32)
        near_z = rows[2:3].astype(BF16).astype(F32)
        gain = (jnp.sum(near_x, axis=1, keepdims=True)
                * jnp.sum(near_y, axis=1, keepdims=True)
                * jnp.sum(near_z, axis=1, keepdims=True))
        tx = banded(near_x)
        ty = banded(near_y)
        r = pl.multiple_of(k * 32, 32)
        fxt[pl.ds(r, 32), :] = tx.astype(BF16)
        fyt[k] = ty.astype(BF16)
        tpose[pl.ds(r, 32), :] = tx
        byt[k] = jnp.concatenate([ty, jnp.zeros((96, 128), F32)], axis=0).T[0:64, :].astype(BF16)
        tz = pltpu.roll(jnp.broadcast_to(near_z, (128, 128)), 113, 1, stride=1, stride_axis=0)
        tz = jnp.where(near, tz, 0.0)
        bzt[k] = tz.astype(BF16)
        fzt[k] = tz.T.astype(BF16)
        m = masks[k]
        mz[pl.ds(pl.multiple_of(k * 16, 16), 16), :] = dot(
            m, bzt[k]) / gain
        part = lane32 - k * 16
        mine = (part >= 0) & (part < 9)
        px = lax.rem(part + 96, 3)
        py = (part + 96) // 3 - 32
        for j, col in enumerate(side_sums(near_x)):
            sums_x = jnp.where(mine & (px == j), col, sums_x)
        for j, col in enumerate(side_sums(near_y)):
            sums_y = jnp.where(mine & (py == j), col, sums_y)
        return sums_x, sums_y

    zero = jnp.zeros((32, 128), F32)
    sums_x, sums_y = lax.fori_loop(0, 6, tables, (zero, zero))
    txs[...] = sums_x
    tys[...] = sums_y
    bxt[:, 0:128] = tpose[0:128, :].T[0:64].astype(BF16)
    bxt[:, 128:256] = tpose[128:256, :].T[0:64].astype(BF16)

    def weigh(q, _):
        parts = []
        for j in range(8):
            parts.append(txs[...] * tys[pl.ds(q * 8 + j, 1), :])
        w = jnp.dot(jnp.concatenate(parts, axis=0), mz[...],
                    preferred_element_type=F32, precision=lax.Precision.HIGHEST)
        low_inv[pl.ds(pl.multiple_of(q * 256, 256), 256), :] = 1.0 / (w + 0.5)
        return 0

    lax.fori_loop(0, 4, weigh, 0)

    def forward_y(k, p):
        cols = jnp.concatenate(
            [wide_a[pl.ds(k * 32 + p * 2 + j, 64, stride=PITCH_A), :].astype(BF16)
             for j in range(2)], axis=1)
        out = dot(fyt[k][:, 0:64], cols).astype(BF16)
        rows_u[p * 64:p * 64 + 32, :] = out[:, 0:128]
        rows_u[p * 64 + 32:p * 64 + 64, :] = out[:, 128:256]

    def backward_y(k, p):
        cols = jnp.concatenate(
            [rows_v[p * 64 + j * 32:p * 64 + j * 32 + 32, :] for j in range(2)], axis=1)
        out = dot(byt[k][:, 0:32], cols)
        for j in range(2):
            r = pl.multiple_of((k * 32 + p * 2 + j) * PITCH_B, 4)
            wide_b[pl.ds(r, 64), :] = out[:, j * 128:j * 128 + 128]

    def middle(k, images):
        covered = masks[k, 4:5, :].astype(F32) > 0.5
        for c in range(4):
            part = slice(c * 256, c * 256 + 256)
            f = dot(rows_u[part, :], fzt[k])
            pic = jnp.where(covered, images[part, :].astype(F32), 0.0)
            rows_r[part, :] = (pic / f).astype(BF16)
        for c in range(4):
            part = slice(c * 256, c * 256 + 256)
            rows_v[part, :] = dot(rows_r[part, :], bzt[k]).astype(BF16)

    def view_step(k, last, images):
        for p in range(16):
            forward_y(k, p)
            backward_y(last, p)
        middle(k, images)

    for step in range(ITERS):
        def pass_x(p, _):
            cols = jnp.concatenate([ext[p * 2], ext[p * 2 + 1]], axis=1)
            out = dot(fxt[:, 0:64], cols)
            for j in range(2):
                r = pl.multiple_of((p * 2 + j) * PITCH_A, 4)
                wide_a[pl.ds(r, 192), :] = out[:, j * 128:j * 128 + 128]
            return 0

        each(X_FACES, lambda d: recv_ext(ext_copy, d))
        lax.fori_loop(8, 24, pass_x, 0, unroll=16)
        for out, side in enumerate((1 - core, core)):
            toward(NOT_X_FACES, out, lambda d: recv_ext(ext_copy, d))
            lax.fori_loop(0, 8, lambda p, c, side=side: pass_x(side * 24 + p, c), 0, unroll=8)

        for p in range(16):
            forward_y(own, p)
        middle(own, img_ref.at[0])

        def own_views(n, _):
            view_step(own + n, own + n - 1, img_ref.at[n])
            return 0

        lax.fori_loop(1, 3, own_views, 0)

        if step == 0:
            for i in range(3):
                img_copy(i).wait()

                def unfold(c, _, i=i):
                    r = pl.multiple_of(c * 64, 64)
                    stay = img_got[i, pl.ds(r, 64), :].astype(F32)
                    move = pltpu.roll(stay, 64, 1)
                    img2[i, pl.ds(r, 64), :] = jnp.where(low_half, stay, move).astype(BF16)
                    img2[i, pl.ds(r + 512, 64), :] = jnp.where(low_half, move, stay).astype(BF16)
                    return 0

                lax.fori_loop(0, 8, unfold, 0, unroll=2)

        def other_views(n, _):
            view_step(oth + n, jnp.where(n == 0, own + 2, oth + n - 1), img2.at[n])
            return 0

        lax.fori_loop(0, 3, other_views, 0)
        for p in range(16):
            backward_y(oth + 2, p)

        def back_x(p, peak):
            pair = [wide_b[pl.ds(p * 2 + j, 192, stride=PITCH_B), :] for j in range(2)]
            hi, lo = split(jnp.concatenate(pair, axis=1))
            th = bxt[:, 0:192]
            out = dot(th, hi) + dot(th, lo)
            for j in range(2):
                part = out[:, j * 128:j * 128 + 128]
                corr[p * 2 + j] = part
                peak = jnp.maximum(peak, part)
            return peak

        def gain_of(peak, slot):
            peak = jnp.max(jnp.max(peak, axis=0, keepdims=True), axis=1, keepdims=True)
            peak = jnp.maximum(peak, 1e-30)
            scale[slot] = jnp.broadcast_to(peak * (1.0 / QMAX), (8, 128))
            return jnp.broadcast_to(QMAX / peak, (16, 128))

        def put(y, x, gain):
            quant[y, x:x + 16, :] = jnp.round(
                corr[y, x:x + 16, :] * gain).astype(jnp.int32).astype(I16)

        if step > 0:
            each(DIRS, lambda d: [c.wait_send() for c in corr_copies(d)])
        zeros = jnp.zeros((64, 128), F32)
        start = lambda d: [c.start() for c in corr_copies(d)]
        for slot, side in enumerate((core, 1 - core)):
            def back_side(p, peak, side=side):
                return back_x(side * 24 + p, peak)

            gain = gain_of(lax.fori_loop(0, 8, back_side, zeros, unroll=8), slot)

            def code_side(y, _, side=side, gain=gain):
                for x in (0, 16, 32, 48):
                    put(side * 48 + y, x, gain)
                return 0

            lax.fori_loop(0, 16, code_side, 0, unroll=4)
            toward(Y_FACES + CORNERS, 1 - slot, start)

        peak = lax.fori_loop(8, 24, back_x, zeros, unroll=8)
        inner = gain_of(peak, 2)

        def code_inner(y, _):
            put(y, 0, inner)
            put(y, 48, inner)
            return 0

        lax.fori_loop(16, 48, code_inner, 0, unroll=4)
        each(X_FACES, lambda d: [c.start() for c in corr_copies(d)])
        each(DIRS, lambda d: ext_copy(d).wait_send())
        each(X_FACES, lambda d: recv_corr(corr_copies, d))

        def factor(index):
            return jnp.broadcast_to(got_scale[index, 0:1, :], (16, 128))

        from_low, from_high = factor(INDEX[(0, -1)]), factor(INDEX[(0, 1)])

        def wide(ref):
            return ref.astype(jnp.int32).astype(F32)

        def finish(y, i=None, s=None, near=None):
            left = corr[y + 16, 16:32, :] + wide(got_x[0, y]) * from_low
            right = corr[y + 16, 32:48, :] + wide(got_x[1, y]) * from_high
            if near is not None:
                left = left + wide(got_y[s, i, 0:16]) * near[1]
                left = left + wide(got_c[s, 0, i]) * near[0]
                right = right + wide(got_y[s, i, 16:32]) * near[1]
                right = right + wide(got_c[s, 1, i]) * near[2]
            total = jnp.concatenate([left, right], axis=0)
            r = pl.multiple_of(y * 32, 32)
            new = joined[pl.ds(r, 32), :] * (total + 0.5) * low_inv[pl.ds(r, 32), :]
            if step + 1 < ITERS:
                joined[pl.ds(r, 32), :] = new
                ext[pl.ds(y + 16, 1), 16:48, :] = new.astype(BF16)[None]
            else:
                flat[pl.ds(y, 32, stride=40), :] = new

        finish(15)
        finish(16)
        for out, side in enumerate((1 - core, core)):
            toward(NOT_X_FACES, out, lambda d: recv_corr(corr_copies, d))
            near = [factor(side * 5 + j) for j in range(3)]

            def edges(i, _, side=side, near=near):
                finish(i + 17 * side, i, side, near)
                return 0

            lax.fori_loop(0, 15, edges, 0, unroll=5)
        if step + 1 < ITERS:
            send_ext()

    def put_out(x, _):
        out_ref[pl.ds(x * 4, 4)] = block[pl.ds(x * 4, 4), 0:32, :]
        return 0

    lax.fori_loop(0, 8, put_out, 0, unroll=2)
    each(DIRS, lambda d: [c.wait_send() for c in corr_copies(d)])


def recv_ext(copy, s):
    copy((-s[0], -s[1])).wait_recv()


def recv_corr(copies, s):
    for c in copies((-s[0], -s[1])):
        c.wait_recv()


def body(fx_size, fy_size, estimate, images, psf, cover_lo, cover_len):
    vmem = pl.BlockSpec(memory_space=pltpu.VMEM)
    smem = pl.BlockSpec(memory_space=pltpu.SMEM)
    anywhere = pl.BlockSpec(memory_space=pltpu.HBM)
    dma = pltpu.SemaphoreType.DMA
    out = pl.pallas_call(
        functools.partial(kernel, fx_size, fy_size),
        out_shape=jax.ShapeDtypeStruct((32, 32, 128), F32),
        in_specs=[anywhere, anywhere, vmem, smem, smem],
        out_specs=vmem,
        scratch_shapes=[
            pltpu.VMEM((32, 40, 128), F32),
            pltpu.VMEM((3, 1024, 128), BF16),
            pltpu.VMEM((3, 512, 128), BF16),
            pltpu.VMEM((3, 512, 128), BF16),
            pltpu.VMEM((64, 64, 128), BF16),
            pltpu.VMEM((1024, 128), F32),
            pltpu.VMEM((3, 1024, 128), BF16),
            pltpu.VMEM((6, 8, 128), F32),
            pltpu.VMEM((6, 16, 128), BF16),
            pltpu.VMEM((64 * PITCH_A, 128), F32),
            pltpu.VMEM((192 * PITCH_B, 128), F32),
            pltpu.VMEM((64, 64, 128), F32),
            pltpu.VMEM((64, 64, 128), I16),
            pltpu.VMEM((2, 32, 16, 128), I16),
            pltpu.VMEM((2, 15, 32, 128), I16),
            pltpu.VMEM((2, 2, 15, 16, 128), I16),
            pltpu.VMEM((3, 8, 128), F32),
            pltpu.VMEM((8, 8, 128), F32),
            pltpu.VMEM((192, 128), BF16),
            pltpu.VMEM((6, 32, 128), BF16),
            pltpu.VMEM((6, 128, 128), BF16),
            pltpu.VMEM((6, 128, 128), BF16),
            pltpu.VMEM((6, 64, 128), BF16),
            pltpu.VMEM((64, 256), BF16),
            pltpu.VMEM((1024, 128), F32),
            pltpu.VMEM((128, 128), F32),
            pltpu.VMEM((32, 128), F32),
            pltpu.VMEM((32, 128), F32),
            pltpu.VMEM((256, 128), F32),
            pltpu.VMEM((1024, 128), BF16),
            pltpu.VMEM((1024, 128), BF16),
            pltpu.VMEM((1024, 128), BF16),
            dma((8,)), dma((8,)), dma((8,)), dma((8,)),
            dma((8,)), dma((8,)), dma((5,)), dma((5,)), dma((2,)),
        ],
        compiler_params=pltpu.CompilerParams(
            collective_id=0, has_side_effects=True, vmem_limit_bytes=40 << 20),
    )(
        *(pltpu.with_memory_space_constraint(a, pltpu.HBM) for a in (
            estimate, images.reshape(3, 1024, 128), psf, cover_lo, cover_len)))
    return out


def solution(mesh):
    return jax.shard_map(
        functools.partial(body, mesh.shape["fx"], mesh.shape["fy"]),
        mesh=mesh,
        in_specs=(
            P("fx", "fy", None),
            P("view", "fx", "fy", None),
            P("view", None, None),
            P("view", None, None),
            P("view", None, None),
        ),
        out_specs=P("fx", "fy", None),
        check_vma=False,
    )
```
